256 devices in a mesh: db: 64 (over x, z, core), pb: 4 (over y).
Axes of the slice: x: 4, y: 4, z: 8, core: 2. Of those that a mesh axis runs over, the one named last changes fastest.
Arguments:
- affinity_tiles: bfloat16 [1024, 16, 128, 128], P('db', None, 'pb'), as said below
- block_ids: int32 [1024, 16], P('db'), may hold values from 0 to 1023, as said below
- valid_counts: int32 [1024], P('db'), may hold values from 4 to 16
- queries: bfloat16 [131072, 512], P('db', 'pb'), may hold values from -6 to 6
Outputs:
- ranked: bfloat16 [131072, 512], P('db', 'pb')
The draws below stay inside these ranges and needn't reach their ends.
Inputs may be any that keep to these rules, and one draw needn't show every extreme that they name: `block_ids`: slot 0 of row block b names b itself. Slots 1 and 2 name blocks held by other indices of db; over the 16 row blocks of one index of db, these slots name blocks of any single other index at most 2 times, and exactly 2 times for some index. Slots 3 and above name blocks no more than 2 blocks outside the range of the row block's own index of db. `affinity_tiles`: tiles in slots at or beyond their row block's count are zero.
All inputs are finite; a program needn't handle non-finite values.
Results may differ from the reference program's by a relative error of at most 0.0034.
Values may be sent and summed in bfloat16 or wider, within the bound.
No kernel may reach another device: no remote copies, remote signals or barrier semaphores. Data moves between devices by JAX's collectives and lax.ppermute only.
A program may use at most 192 MiB of HBM per device.

```python
import math
import jax
import jax.numpy as jnp
from jax import lax

RB_DEV = 16
TILES = 16
BLK = 128
QCOL = 512
EDGE = 2
ITERS = 2
NBLK = 1024
ROWS = 131072
CAP = 2
N_DB = 64


def block_layout(key):
    base_key = jax.random.fold_in(key, 4101)

    def one_device(device):
        subkeys = jax.random.split(jax.random.fold_in(base_key, device), 6)
        first_block = device * RB_DEV
        own_blocks = first_block + jnp.arange(RB_DEV, dtype=jnp.int32)
        offsets = jax.random.permutation(subkeys[0], N_DB - 1).astype(jnp.int32) + 1
        grouping = jnp.arange(2 * RB_DEV, dtype=jnp.int32) // CAP
        peer_index = (device + jnp.take(offsets, grouping)) % N_DB
        far_blocks = peer_index * RB_DEV + jax.random.randint(subkeys[1], (2 * RB_DEV,), 0, RB_DEV, dtype=jnp.int32)
        lowest = jnp.maximum(0, first_block - EDGE)
        highest = jnp.minimum(NBLK - 1, first_block + RB_DEV - 1 + EDGE)
        near_blocks = lowest + jax.random.randint(subkeys[2], (RB_DEV, TILES - 3), 0, highest - lowest + 1, dtype=jnp.int32)
        lower_edge = jnp.maximum(0, first_block - 1 - jax.random.randint(subkeys[3], (), 0, EDGE, dtype=jnp.int32))
        upper_edge = jnp.minimum(NBLK - 1, first_block + RB_DEV + jax.random.randint(subkeys[4], (), 0, EDGE, dtype=jnp.int32))
        near_blocks = near_blocks.at[0, 0].set(lower_edge).at[RB_DEV - 1, 0].set(upper_edge)
        block_rows = jnp.concatenate([own_blocks[:, None], far_blocks.reshape(RB_DEV, 2), near_blocks], axis=1)
        counts = jax.random.randint(subkeys[5], (RB_DEV,), 4, TILES + 1, dtype=jnp.int32)
        counts = counts.at[0].set(TILES).at[RB_DEV - 1].set(4)
        return (block_rows, counts)
    block_rows, counts = jax.vmap(one_device)(jnp.arange(N_DB, dtype=jnp.int32))
    return (block_rows.reshape(NBLK, TILES), counts.reshape(NBLK))


def draw_block_ids(key, part):
    return block_layout(key)[0]


def draw_valid_counts(key, part):
    return block_layout(key)[1]


def draw_affinity_tiles(key, part):
    counts = block_layout(key)[1]
    spread = 0.7 / math.sqrt(TILES * BLK)
    value_key = jax.random.fold_in(key, 9173)
    tile_shape = (NBLK, TILES, BLK, BLK)
    values = jax.random.normal(value_key, tile_shape, jnp.float32) * spread
    live_slots = (jnp.arange(TILES, dtype=jnp.int32)[None, :] < counts[:, None]).astype(jnp.float32)
    return (values * live_slots[:, :, None, None]).astype(jnp.bfloat16)


def block_levels(stream_key, shape, shards, least, largest):
    def one(axis_at, shards_of):
        steps = jax.random.uniform(jax.random.fold_in(jax.random.fold_in(stream_key, 6), axis_at), (shards_of,), jnp.float32, least / len(shards), largest / len(shards))
        return jnp.repeat(jnp.exp(steps), shape[axis_at] // shards_of).reshape((-1,) + (1,) * (len(shape) - axis_at - 1))

    loudness = one(*shards[0])
    for cut in shards[1:]:
        loudness = loudness * one(*cut)
    return loudness


def gaussian(own_key, extent, scale, most, cuts=(), kind=jnp.bfloat16):
    level = block_levels(own_key, extent, cuts, -0.22, 0.18) if cuts else 1.0
    result = jax.random.normal(own_key, extent, jnp.float32) * scale * level
    return jnp.minimum(jnp.maximum(result, -most), most).astype(kind)


def setup_inputs(seed: int = 0) -> dict:
    keys = jax.random.split(jax.random.key(seed), 5)
    return {
        "affinity_tiles": draw_affinity_tiles(jax.random.fold_in(keys[4], 71), 0),
        "block_ids": draw_block_ids(jax.random.fold_in(keys[4], 71), 0),
        "valid_counts": draw_valid_counts(jax.random.fold_in(keys[4], 71), 0),
        "queries": gaussian(keys[3], (ROWS, QCOL), 1.0, 6.0, ((0, 64), (1, 4))),
    }


def reference(affinity_tiles, block_ids, valid_counts, queries):
    block_total = block_ids.shape[0]
    block_size = affinity_tiles.shape[2]
    query_cols = queries.shape[1]
    slot_mask = (jnp.arange(TILES, dtype=jnp.int32)[None, :] < valid_counts[:, None]).astype(jnp.float32)
    ranking = queries.reshape(block_total, block_size, query_cols)
    prior_field = ranking.astype(jnp.float32)
    group_count = block_total // RB_DEV
    grouped_tiles = affinity_tiles.reshape(group_count, RB_DEV, TILES, block_size, block_size)
    grouped_ids = block_ids.reshape(group_count, RB_DEV, TILES)
    grouped_mask = slot_mask.reshape(group_count, RB_DEV, TILES)
    for step_index in range(ITERS):
        def group_product(pieces, current=ranking):
            tile_group, id_group, mask_group = pieces
            panels = jnp.take(current, id_group, axis=0).astype(jnp.float32)
            weights = tile_group.astype(jnp.float32) * mask_group[:, :, None, None]
            return jnp.einsum("rtij,rtjq->riq", weights, panels)
        gathered = lax.map(group_product, (grouped_tiles, grouped_ids, grouped_mask))
        summed = gathered.reshape(block_total, block_size, query_cols)
        ranking = (0.99 * summed + prior_field).astype(jnp.bfloat16)
    return ranking.reshape(block_total * block_size, query_cols)
```

```python
import jax
import jax.numpy as jnp
from jax import lax
from jax.experimental import pallas as pl
from jax.experimental.pallas import tpu as pltpu
from jax.sharding import PartitionSpec as P

EDGE = 2
ITERS = 2
NEAR = (0,) + tuple(range(3, 16))


def rows_to_pieces(wide, pieces_ref, blocks, size, owners):
    cols = wide.shape[1]
    for k in range(owners):
        for part in range(size // owners):
            rows = wide[pl.ds(part * owners + k, blocks, stride=size), :]
            pieces_ref[k * blocks : (k + 1) * blocks, part * cols : (part + 1) * cols] = rows.astype(
                pieces_ref.dtype
            )


def split_blocks(queries, blocks, size, owners):
    cols = queries.shape[1]

    def kernel(q_ref, pieces_ref, wide):
        wide[...] = q_ref[...].astype(jnp.float32)
        rows_to_pieces(wide, pieces_ref, blocks, size, owners)

    return pl.pallas_call(
        kernel,
        out_shape=jax.ShapeDtypeStruct((owners * blocks, size // owners * cols), queries.dtype),
        in_specs=[pl.BlockSpec(memory_space=pltpu.VMEM)],
        out_specs=pl.BlockSpec(memory_space=pltpu.VMEM),
        scratch_shapes=[pltpu.VMEM(queries.shape, jnp.float32)],
        name="split_blocks",
    )(queries)


def select_pieces(wanted, pieces):
    slots, devices = wanted.shape
    block_total, width = pieces.shape

    def kernel(wanted_ref, pieces_ref, out_ref, hits):
        for d in range(devices):
            ids = jnp.broadcast_to(wanted_ref[:, d : d + 1], (slots, block_total))
            column = lax.broadcasted_iota(jnp.int32, (slots, block_total), 1)
            hits[d * slots : (d + 1) * slots, :] = jnp.where(ids == column, 1.0, 0.0).astype(hits.dtype)
        step = 256

        @pl.loop(0, devices * slots // step)
        def _(i):
            rows = pl.ds(pl.multiple_of(i * step, step), step)
            out_ref[rows, :] = jnp.dot(
                hits[rows, :], pieces_ref[...], preferred_element_type=jnp.float32
            ).astype(out_ref.dtype)

    return pl.pallas_call(
        kernel,
        out_shape=jax.ShapeDtypeStruct((devices * slots, width), pieces.dtype),
        in_specs=[pl.BlockSpec(memory_space=pltpu.VMEM)] * 2,
        out_specs=pl.BlockSpec(memory_space=pltpu.VMEM),
        scratch_shapes=[pltpu.VMEM((devices * slots, block_total), jnp.bfloat16)],
        compiler_params=pltpu.CompilerParams(vmem_limit_bytes=32 << 20),
        cost_estimate=pl.CostEstimate(
            flops=2 * devices * slots * block_total * width, bytes_accessed=2 << 20, transcendentals=0
        ),
        name="select_pieces",
    )(wanted, pieces)


def near_product(near_index, counts, tiles, low, own, high):
    blocks, slots, rows, size = tiles.shape
    cols = own.shape[2]
    group = 4

    def kernel(index_ref, count_ref, tiles_ref, low_ref, own_ref, high_ref, out_ref, panels):
        step = pl.program_id(0)

        @pl.when(step == 0)
        def _():
            panels[:EDGE] = low_ref[...]
            panels[EDGE : EDGE + blocks] = own_ref[...]
            panels[EDGE + blocks :] = high_ref[...]

        for r in range(group):
            b = step * group + r
            total = jnp.zeros((rows, cols), jnp.float32)
            for first in range(0, len(NEAR), 2):
                pair = NEAR[first : first + 2]
                left = [
                    jnp.where(t < count_ref[b], tiles_ref[r, t], jnp.zeros((rows, size), tiles.dtype))
                    for t in pair
                ]
                right = [panels[index_ref[b, t]] for t in pair]
                total += jnp.dot(
                    jnp.concatenate(left, axis=1),
                    jnp.concatenate(right, axis=0),
                    preferred_element_type=jnp.float32,
                )
            out_ref[r] = total

    whole = pl.BlockSpec(memory_space=pltpu.VMEM)
    return pl.pallas_call(
        kernel,
        out_shape=jax.ShapeDtypeStruct((blocks, rows, cols), jnp.float32),
        grid_spec=pltpu.PrefetchScalarGridSpec(
            num_scalar_prefetch=2,
            grid=(blocks // group,),
            in_specs=[
                pl.BlockSpec((group, slots, rows, size), lambda i, *_: (i, 0, 0, 0)),
                whole,
                whole,
                whole,
            ],
            out_specs=pl.BlockSpec((group, rows, cols), lambda i, *_: (i, 0, 0)),
            scratch_shapes=[pltpu.VMEM((blocks + 2 * EDGE, size, cols), own.dtype)],
        ),
        compiler_params=pltpu.CompilerParams(vmem_limit_bytes=32 << 20),
        cost_estimate=pl.CostEstimate(
            flops=2 * blocks * len(NEAR) * rows * size * cols, bytes_accessed=9 << 20, transcendentals=0
        ),
        name="near_product",
    )(near_index, counts, tiles, low, own, high)


def add_far(counts, far_tiles, arrived, partial, queries, owners, split):
    blocks, _, size, _ = far_tiles.shape
    cols = queries.shape[1]
    far = arrived.shape[0] // owners

    def kernel(count_ref, tiles_ref, arrived_ref, partial_ref, q_ref, *rest):
        if split:
            out_ref, pieces_ref, upper, lower, wide = rest
        else:
            out_ref, upper, lower = rest
        upper[...] = arrived_ref[:, :cols].astype(jnp.float32)
        lower[...] = arrived_ref[:, cols:].astype(jnp.float32)
        for b in range(blocks):
            left, right = [], []
            for s in range(2):
                j = 2 * b + s
                left.append(
                    jnp.where(s + 1 < count_ref[b], tiles_ref[b, s], jnp.zeros((size, size), far_tiles.dtype))
                )
                for half in (upper, lower):
                    right.append(half[pl.ds(j, owners, stride=far), :].astype(far_tiles.dtype))
            total = partial_ref[b] + jnp.dot(
                jnp.concatenate(left, axis=1),
                jnp.concatenate(right, axis=0),
                preferred_element_type=jnp.float32,
            )
            rows = slice(b * size, (b + 1) * size)
            result = (0.99 * total + q_ref[rows, :].astype(jnp.float32)).astype(out_ref.dtype)
            out_ref[rows, :] = result
            if split:
                wide[rows, :] = result.astype(jnp.float32)
        if split:
            rows_to_pieces(wide, pieces_ref, blocks, size, owners)

    out_shape = [jax.ShapeDtypeStruct(queries.shape, queries.dtype)]
    scratch = [pltpu.VMEM((owners * far, cols), jnp.float32)] * 2
    if split:
        out_shape.append(jax.ShapeDtypeStruct((owners * blocks, size // owners * cols), queries.dtype))
        scratch.append(pltpu.VMEM(queries.shape, jnp.float32))
    return pl.pallas_call(
        kernel,
        out_shape=out_shape,
        in_specs=[pl.BlockSpec(memory_space=pltpu.SMEM)] + [pl.BlockSpec(memory_space=pltpu.VMEM)] * 4,
        out_specs=[pl.BlockSpec(memory_space=pltpu.VMEM)] * len(out_shape),
        scratch_shapes=scratch,
        compiler_params=pltpu.CompilerParams(vmem_limit_bytes=32 << 20),
        cost_estimate=pl.CostEstimate(
            flops=4 * blocks * size * size * cols, bytes_accessed=4 << 20, transcendentals=0
        ),
        name="add_far",
    )(counts, far_tiles, arrived, partial, queries)


def exchange(array, axis, parts):
    shape = array.shape
    array = array.reshape((parts, shape[0] // parts) + shape[1:])
    return lax.all_to_all(array, axis, split_axis=0, concat_axis=0, tiled=True).reshape(shape)


def on_device(affinity_tiles, block_ids, valid_counts, queries):
    blocks, slots = block_ids.shape
    size = affinity_tiles.shape[3]
    cols = queries.shape[1]
    owners = lax.axis_size("db")
    first_block = lax.axis_index("db") * blocks
    full_tiles = lax.all_gather(affinity_tiles, "pb", axis=2, tiled=True)
    far_tiles = full_tiles[:, 1:3]
    near_index = jnp.clip(block_ids - first_block + EDGE, 0, blocks + 2 * EDGE - 1)
    named = jnp.broadcast_to(block_ids[:, 1:3].reshape(1, 1, -1), (owners, 1, 2 * blocks))
    wanted = lax.all_to_all(named, "db", split_axis=0, concat_axis=0, tiled=True)
    wanted = wanted.reshape(owners, 2 * blocks).T
    up = [(i, i + 1) for i in range(owners - 1)]
    down = [(i + 1, i) for i in range(owners - 1)]
    ranking = queries
    pieces = split_blocks(queries, blocks, size, owners)
    for step in range(ITERS):
        own = ranking.reshape(blocks, size, cols)
        held = exchange(pieces, "db", owners)
        low = lax.ppermute(own[blocks - EDGE :], "db", up)
        high = lax.ppermute(own[:EDGE], "db", down)
        arrived = exchange(select_pieces(wanted, held), "db", owners)
        partial = near_product(near_index, valid_counts, full_tiles, low, own, high)
        done = add_far(valid_counts, far_tiles, arrived, partial, queries, owners, step < ITERS - 1)
        ranking = done[0]
        pieces = done[-1]
    return ranking


def solution(mesh):
    return jax.shard_map(
        on_device,
        mesh=mesh,
        in_specs=(P("db", None, "pb", None), P("db", None), P("db"), P("db", "pb")),
        out_specs=P("db", "pb"),
        check_vma=False,
    )
```

```python
import jax
import jax.numpy as jnp
from jax import lax
from jax.experimental import pallas as pl
from jax.experimental.pallas import tpu as pltpu
from jax.sharding import PartitionSpec as P

EDGE = 2
ITERS = 2
BASE = 256
FAR = (1, 2)
LOW = tuple(range(1, 9))
HIGH = tuple(range(9, 16)) + (0,)
VMEM = pl.BlockSpec(memory_space=pltpu.VMEM)
SMEM = pl.BlockSpec(memory_space=pltpu.SMEM)


def rows_to_pieces(wide, pieces_ref, blocks, size, owners):
    for k in range(owners):
        for part in range(size // owners):
            rows = wide[pl.ds(part * owners + k, blocks, stride=size), :]
            pieces_ref[k, part * blocks : (part + 1) * blocks, :] = rows.astype(pieces_ref.dtype)


def split_blocks(queries, digits, blocks, size, owners):
    cols = queries.shape[1]
    rows = size // owners * blocks

    def kernel(q_ref, digits_ref, pieces_ref, wide):
        wide[...] = q_ref[...].astype(jnp.float32)
        rows_to_pieces(wide, pieces_ref, blocks, size, owners)
        for k in range(owners):
            pieces_ref[k, rows:, :] = jnp.broadcast_to(digits_ref[...], (8, cols)).astype(pieces_ref.dtype)

    return pl.pallas_call(
        kernel,
        out_shape=jax.ShapeDtypeStruct((owners, rows + 8, cols), queries.dtype),
        in_specs=[VMEM, VMEM],
        out_specs=VMEM,
        scratch_shapes=[pltpu.VMEM(queries.shape, jnp.float32)],
        name="split_blocks",
    )(queries, digits)


def select_pieces(held, slots, wanted=None):
    devices, height, cols = held.shape
    blocks = height // 16 * 8
    parts = 2
    block_total = devices * blocks
    group = 8

    def kernel(held_ref, *rest):
        if wanted is None:
            out_ref, wanted_out, flat = rest
            digits = held_ref[:, parts * blocks :, :].astype(jnp.float32)[:, 0, :].T
            ids = (digits[:slots] * BASE + digits[slots : 2 * slots]).astype(jnp.int32)
            wanted_out[...] = ids
        else:
            wanted_ref, out_ref, flat = rest
            ids = wanted_ref[...]
        for s in range(devices):
            for part in range(parts):
                flat[s * blocks : (s + 1) * blocks, part * cols : (part + 1) * cols] = held_ref[
                    s, part * blocks : (part + 1) * blocks, :
                ]
        column = lax.broadcasted_iota(jnp.int32, (slots, block_total), 1)
        for first in range(0, devices, group):
            hits = [
                jnp.where(
                    jnp.broadcast_to(ids[:, d : d + 1], (slots, block_total)) == column, 1.0, 0.0
                ).astype(held.dtype)
                for d in range(first, first + group)
            ]
            out_ref[first * slots : (first + group) * slots, :] = jnp.dot(
                jnp.concatenate(hits, axis=0), flat[...], preferred_element_type=jnp.float32
            ).astype(out_ref.dtype)

    out_shape = [jax.ShapeDtypeStruct((devices * slots, parts * cols), held.dtype)]
    if wanted is None:
        out_shape.append(jax.ShapeDtypeStruct((slots, devices), jnp.int32))
    operands = (held,) if wanted is None else (held, wanted)
    return pl.pallas_call(
        kernel,
        out_shape=out_shape,
        in_specs=[VMEM] * len(operands),
        out_specs=[VMEM] * len(out_shape),
        scratch_shapes=[pltpu.VMEM((block_total, parts * cols), held.dtype)],
        compiler_params=pltpu.CompilerParams(vmem_limit_bytes=32 << 20),
        cost_estimate=pl.CostEstimate(
            flops=2 * devices * slots * block_total * parts * cols, bytes_accessed=2 << 20, transcendentals=0
        ),
        name="select_pieces",
    )(*operands)


def near_product(near_index, counts, quarters, low, own, high):
    blocks, _, rows, size = quarters[0][0].shape
    cols = own.shape[2]
    group = 4
    number = len(quarters)
    near = [(half, place, t) for half, names in enumerate((LOW, HIGH)) for place, t in enumerate(names)]
    near = [entry for entry in near if entry[2] not in FAR]

    def kernel(index_ref, count_ref, *refs):
        tiles = [refs[2 * n : 2 * n + 2] for n in range(number)]
        low_ref, own_ref, high_ref, out_ref, panels = refs[2 * number :]
        step = pl.program_id(0)

        @pl.when(step == 0)
        def _():
            panels[:EDGE] = low_ref[...]
            panels[EDGE : EDGE + blocks] = own_ref[...]
            panels[EDGE + blocks :] = high_ref[...]

        for r in range(group):
            b = step * group + r
            total = jnp.zeros((number * rows, cols), jnp.float32)
            for first in range(0, len(near), 2):
                left, right = [], []
                for half, place, t in near[first : first + 2]:
                    tile = jnp.concatenate([pair[half][r, place] for pair in tiles], axis=0)
                    left.append(jnp.where(t < count_ref[b], tile, jnp.zeros_like(tile)))
                    right.append(panels[index_ref[b, t]])
                total += jnp.dot(
                    jnp.concatenate(left, axis=1),
                    jnp.concatenate(right, axis=0),
                    preferred_element_type=jnp.float32,
                )
            out_ref[r] = total

    return pl.pallas_call(
        kernel,
        out_shape=jax.ShapeDtypeStruct((blocks, number * rows, cols), jnp.float32),
        grid_spec=pltpu.PrefetchScalarGridSpec(
            num_scalar_prefetch=2,
            grid=(blocks // group,),
            in_specs=[
                pl.BlockSpec((group, half.shape[1], rows, size), lambda i, *_: (i, 0, 0, 0))
                for pair in quarters
                for half in pair
            ]
            + [VMEM] * 3,
            out_specs=pl.BlockSpec((group, number * rows, cols), lambda i, *_: (i, 0, 0)),
            scratch_shapes=[pltpu.VMEM((blocks + 2 * EDGE, size, cols), own.dtype)],
        ),
        compiler_params=pltpu.CompilerParams(vmem_limit_bytes=32 << 20),
        cost_estimate=pl.CostEstimate(
            flops=2 * blocks * len(near) * number * rows * size * cols,
            bytes_accessed=number << 21,
            transcendentals=0,
        ),
        name="near_product",
    )(near_index, counts, *[half for pair in quarters for half in pair], low, own, high)


def add_far(offsets, counts, far_tiles, arrived, partials, queries, owners, split):
    blocks, _, rows, size = far_tiles[0].shape
    cols = queries.shape[1]
    far = arrived.shape[0] // owners
    number = len(far_tiles)

    def kernel(offset_ref, count_ref, *refs):
        tiles = refs[:number]
        arrived_ref = refs[number]
        partial_refs = refs[number + 1 : number + 1 + len(partials)]
        q_ref, out_ref, *rest = refs[number + 1 + len(partials) :]
        if split:
            pieces_ref, upper, lower, wide = rest
        else:
            upper, lower = rest
        upper[...] = arrived_ref[:, :cols].astype(jnp.float32)
        lower[...] = arrived_ref[:, cols:].astype(jnp.float32)
        for b in range(blocks):
            left, right = [], []
            for s, t in enumerate(FAR):
                tile = jnp.concatenate([ref[b, s] for ref in tiles], axis=0)
                left.append(jnp.where(t < count_ref[b], tile, jnp.zeros_like(tile)))
                for half in (upper, lower):
                    right.append(half[pl.ds(2 * b + s, owners, stride=far), :].astype(queries.dtype))
            total = jnp.concatenate([ref[b] for ref in partial_refs], axis=0) + jnp.dot(
                jnp.concatenate(left, axis=1),
                jnp.concatenate(right, axis=0),
                preferred_element_type=jnp.float32,
            )
            for n in range(number):
                place = pl.ds(pl.multiple_of(b * size + offset_ref[n], rows), rows)
                result = 0.99 * total[n * rows : (n + 1) * rows] + q_ref[place, :].astype(jnp.float32)
                result = result.astype(out_ref.dtype)
                out_ref[place, :] = result
                if split:
                    wide[place, :] = result.astype(jnp.float32)
        if split:
            rows_to_pieces(wide, pieces_ref, blocks, size, owners)

    out_shape = [jax.ShapeDtypeStruct(queries.shape, queries.dtype)]
    out_specs = [pl.BlockSpec(queries.shape, lambda i, *_: (0, 0))]
    scratch = [pltpu.VMEM((owners * far, cols), jnp.float32)] * 2
    if split:
        shape = (owners, size // owners * blocks, cols)
        out_shape.append(jax.ShapeDtypeStruct(shape, queries.dtype))
        out_specs.append(pl.BlockSpec(shape, lambda i, *_: (0, 0, 0)))
        scratch.append(pltpu.VMEM(queries.shape, jnp.float32))
    return pl.pallas_call(
        kernel,
        out_shape=out_shape,
        grid_spec=pltpu.PrefetchScalarGridSpec(
            num_scalar_prefetch=2,
            grid=(1,),
            in_specs=[pl.BlockSpec((blocks, len(FAR), rows, size), lambda i, *_: (0, 0, 0, 0))] * number
            + [VMEM] * (2 + len(partials)),
            out_specs=out_specs,
            scratch_shapes=scratch,
        ),
        compiler_params=pltpu.CompilerParams(vmem_limit_bytes=32 << 20),
        cost_estimate=pl.CostEstimate(
            flops=4 * blocks * size * size * cols, bytes_accessed=4 << 20, transcendentals=0
        ),
        name="add_far",
    )(offsets, counts, *far_tiles, arrived, *partials, queries)


def gather_rows(tiles):
    count = lax.axis_size("pb")
    up = [(i, (i + 1) % count) for i in range(count)]
    down = [((i + 1) % count, i) for i in range(count)]
    low = tiles[:, LOW[0] : LOW[-1] + 1]
    high = jnp.concatenate([tiles[:, HIGH[0] :], tiles[:, :1]], axis=1)
    before_low = lax.ppermute(low, "pb", up)
    after_high = lax.ppermute(high, "pb", down)
    before_high = lax.ppermute(high, "pb", up)
    after_low = lax.ppermute(low, "pb", down)
    far_low = lax.ppermute(before_low, "pb", up)
    far_high = lax.ppermute(after_high, "pb", down)
    return [(low, high), (before_low, before_high), (after_low, after_high), (far_low, far_high)]


def on_device(affinity_tiles, block_ids, valid_counts, queries):
    blocks, slots = block_ids.shape
    rows, size = affinity_tiles.shape[2:]
    cols = queries.shape[1]
    owners = lax.axis_size("db")
    first_block = lax.axis_index("db") * blocks
    quarters = gather_rows(affinity_tiles)
    far_tiles = [pair[0] for pair in quarters]
    place = lax.axis_index("pb")
    offsets = jnp.stack([(place + shift) % lax.axis_size("pb") * rows for shift in (0, -1, 1, 2)])
    near_index = jnp.clip(block_ids - first_block + EDGE, 0, blocks + 2 * EDGE - 1)
    far = block_ids[:, FAR[0] : FAR[-1] + 1].reshape(1, -1)
    slots = far.shape[1]
    digits = jnp.concatenate([far // BASE, far % BASE], axis=1).astype(jnp.float32)
    digits = jnp.pad(digits, ((0, 0), (0, cols - 2 * slots)))
    up = [(i, i + 1) for i in range(owners - 1)]
    down = [(i + 1, i) for i in range(owners - 1)]
    ranking, wanted = queries, None
    pieces = split_blocks(queries, digits, blocks, size, owners)
    for step in range(ITERS):
        own = ranking.reshape(blocks, size, cols)
        held = lax.all_to_all(pieces, "db", split_axis=0, concat_axis=0, tiled=True)
        low = lax.ppermute(own[blocks - EDGE :], "db", up)
        high = lax.ppermute(own[:EDGE], "db", down)
        if wanted is None:
            chosen, wanted = select_pieces(held, slots)
        else:
            (chosen,) = select_pieces(held, slots, wanted)
        arrived = lax.all_to_all(
            chosen.reshape(owners, slots, -1), "db", split_axis=0, concat_axis=0, tiled=True
        ).reshape(chosen.shape)
        partials = [
            near_product(near_index, valid_counts, part, low, own, high)
            for part in ([quarters[:3], quarters[3:]] if step == 0 else [quarters])
        ]
        done = add_far(offsets, valid_counts, far_tiles, arrived, partials, queries, owners, step < ITERS - 1)
        ranking = done[0]
        pieces = done[-1]
    return ranking


def solution(mesh):
    return jax.shard_map(
        on_device,
        mesh=mesh,
        in_specs=(P("db", None, "pb", None), P("db", None), P("db"), P("db", "pb")),
        out_specs=P("db", "pb"),
        check_vma=False,
    )
```

```python
import jax
import jax.numpy as jnp
from jax import lax
from jax.experimental import pallas as pl
from jax.experimental.pallas import tpu as pltpu
from jax.sharding import PartitionSpec as P

EDGE = 2
ITERS = 2
BASE = 256
FAR = (1, 2)
LIMIT = 12 << 20
VMEM = pl.BlockSpec(memory_space=pltpu.VMEM)
SMEM = pl.BlockSpec(memory_space=pltpu.SMEM)


def rows_to_pieces(wide, pieces_ref, blocks, size, owners):
    for k in range(owners):
        for part in range(size // owners):
            rows = wide[pl.ds(part * owners + k, blocks, stride=size), :]
            pieces_ref[k, part * blocks : (part + 1) * blocks, :] = rows.astype(pieces_ref.dtype)


def split_blocks(queries, digits, blocks, size, owners):
    cols = queries.shape[1]
    rows = size // owners * blocks

    def kernel(q_ref, digits_ref, pieces_ref, wide):
        wide[...] = q_ref[...].astype(jnp.float32)
        rows_to_pieces(wide, pieces_ref, blocks, size, owners)
        for k in range(owners):
            pieces_ref[k, rows:, :] = jnp.broadcast_to(digits_ref[...], (8, cols)).astype(pieces_ref.dtype)

    return pl.pallas_call(
        kernel,
        out_shape=jax.ShapeDtypeStruct((owners, rows + 8, cols), queries.dtype),
        in_specs=[VMEM, VMEM],
        out_specs=VMEM,
        scratch_shapes=[pltpu.VMEM(queries.shape, jnp.float32)],
        name="split_blocks",
    )(queries, digits)


def select_pieces(held, slots, wanted, after):
    devices, height, cols = held.shape
    blocks = height // 16 * 8
    parts = 2
    block_total = devices * blocks
    group = 8

    def kernel(held_ref, *rest):
        rest = rest[len(after) :]
        if wanted is None:
            out_ref, wanted_out, flat = rest
            digits = held_ref[:, parts * blocks :, :].astype(jnp.float32)[:, 0, :].T
            ids = (digits[:slots] * BASE + digits[slots : 2 * slots]).astype(jnp.int32)
            wanted_out[...] = ids
        else:
            wanted_ref, out_ref, flat = rest
            ids = wanted_ref[...]
        for s in range(devices):
            for part in range(parts):
                flat[s * blocks : (s + 1) * blocks, part * cols : (part + 1) * cols] = held_ref[
                    s, part * blocks : (part + 1) * blocks, :
                ]
        column = lax.broadcasted_iota(jnp.int32, (slots, block_total), 1)
        for first in range(0, devices, group):
            hits = [
                jnp.where(
                    jnp.broadcast_to(ids[:, d : d + 1], (slots, block_total)) == column, 1.0, 0.0
                ).astype(held.dtype)
                for d in range(first, first + group)
            ]
            out_ref[first * slots : (first + group) * slots, :] = jnp.dot(
                jnp.concatenate(hits, axis=0), flat[...], preferred_element_type=jnp.float32
            ).astype(out_ref.dtype)

    out_shape = [jax.ShapeDtypeStruct((devices * slots, parts * cols), held.dtype)]
    if wanted is None:
        out_shape.append(jax.ShapeDtypeStruct((slots, devices), jnp.int32))
    operands = () if wanted is None else (wanted,)
    return pl.pallas_call(
        kernel,
        out_shape=out_shape,
        in_specs=[VMEM] + [pl.BlockSpec(memory_space=pl.ANY)] * len(after) + [VMEM] * len(operands),
        out_specs=[VMEM] * len(out_shape),
        scratch_shapes=[pltpu.VMEM((block_total, parts * cols), held.dtype)],
        compiler_params=pltpu.CompilerParams(vmem_limit_bytes=LIMIT),
        cost_estimate=pl.CostEstimate(
            flops=2 * devices * slots * block_total * parts * cols, bytes_accessed=2 << 20, transcendentals=0
        ),
        name="select_pieces",
    )(held, *after, *operands)


def near_product(near_index, counts, tiles, panels):
    blocks, slots, rows, size = tiles.shape
    reach, _, cols = panels[0].shape
    number = len(panels)
    group = 4
    near = [t for t in range(slots) if t not in FAR]

    def kernel(index_ref, count_ref, tiles_ref, *refs):
        panel_refs, out_refs = refs[:number], refs[number:]
        step = pl.program_id(0)
        for r in range(group):
            b = step * group + r
            total = jnp.zeros((rows, number * cols), jnp.float32)
            for first in range(0, len(near), 2):
                left, right = [], []
                for t in near[first : first + 2]:
                    tile = tiles_ref[r, t]
                    left.append(jnp.where(t < count_ref[b], tile, jnp.zeros_like(tile)))
                    right.append(jnp.concatenate([ref[index_ref[b, t]] for ref in panel_refs], axis=1))
                total += jnp.dot(
                    jnp.concatenate(left, axis=1),
                    jnp.concatenate(right, axis=0),
                    preferred_element_type=jnp.float32,
                )
            for n in range(number):
                out_refs[n][r] = total[:, n * cols : (n + 1) * cols]

    out_shape = jax.ShapeDtypeStruct((blocks, rows, cols), jnp.float32)
    return pl.pallas_call(
        kernel,
        out_shape=[out_shape] * number,
        grid_spec=pltpu.PrefetchScalarGridSpec(
            num_scalar_prefetch=2,
            grid=(blocks // group,),
            in_specs=[pl.BlockSpec((group, slots, rows, size), lambda i, *_: (i, 0, 0, 0))] + [VMEM] * number,
            out_specs=[pl.BlockSpec((group, rows, cols), lambda i, *_: (i, 0, 0))] * number,
        ),
        compiler_params=pltpu.CompilerParams(vmem_limit_bytes=LIMIT),
        cost_estimate=pl.CostEstimate(
            flops=2 * blocks * len(near) * number * rows * size * cols,
            bytes_accessed=6 << 20,
            transcendentals=0,
        ),
        name="near_product",
    )(near_index, counts, tiles, *panels)


def add_far(offsets, counts, far_tiles, arrived, partials, queries, owners, split):
    blocks, _, rows, size = far_tiles[0].shape
    cols = queries.shape[1]
    far = arrived.shape[0] // owners
    number = len(far_tiles)

    def kernel(offset_ref, count_ref, *refs):
        tiles = refs[:number]
        arrived_ref = refs[number]
        partial_refs = refs[number + 1 : number + 1 + len(partials)]
        q_ref, out_ref, *rest = refs[number + 1 + len(partials) :]
        if split:
            pieces_ref, upper, lower, wide = rest
        else:
            upper, lower = rest
        upper[...] = arrived_ref[:, :cols].astype(jnp.float32)
        lower[...] = arrived_ref[:, cols:].astype(jnp.float32)
        for b in range(blocks):
            left, right = [], []
            for s, t in enumerate(FAR):
                tile = jnp.concatenate([ref[b, s] for ref in tiles], axis=0)
                left.append(jnp.where(t < count_ref[b], tile, jnp.zeros_like(tile)))
                for half in (upper, lower):
                    right.append(half[pl.ds(2 * b + s, owners, stride=far), :].astype(queries.dtype))
            total = jnp.concatenate([ref[b] for ref in partial_refs], axis=0) + jnp.dot(
                jnp.concatenate(left, axis=1),
                jnp.concatenate(right, axis=0),
                preferred_element_type=jnp.float32,
            )
            for n in range(number):
                place = pl.ds(pl.multiple_of(b * size + offset_ref[n], rows), rows)
                result = 0.99 * total[n * rows : (n + 1) * rows] + q_ref[place, :].astype(jnp.float32)
                result = result.astype(out_ref.dtype)
                out_ref[place, :] = result
                if split:
                    wide[place, :] = result.astype(jnp.float32)
        if split:
            rows_to_pieces(wide, pieces_ref, blocks, size, owners)

    out_shape = [jax.ShapeDtypeStruct(queries.shape, queries.dtype)]
    out_specs = [pl.BlockSpec(queries.shape, lambda i, *_: (0, 0))]
    scratch = [pltpu.VMEM((owners * far, cols), jnp.float32)] * 2
    if split:
        shape = (owners, size // owners * blocks, cols)
        out_shape.append(jax.ShapeDtypeStruct(shape, queries.dtype))
        out_specs.append(pl.BlockSpec(shape, lambda i, *_: (0, 0, 0)))
        scratch.append(pltpu.VMEM(queries.shape, jnp.float32))
    return pl.pallas_call(
        kernel,
        out_shape=out_shape,
        grid_spec=pltpu.PrefetchScalarGridSpec(
            num_scalar_prefetch=2,
            grid=(1,),
            in_specs=[VMEM] * (number + 2 + len(partials)),
            out_specs=out_specs,
            scratch_shapes=scratch,
        ),
        compiler_params=pltpu.CompilerParams(vmem_limit_bytes=LIMIT),
        cost_estimate=pl.CostEstimate(
            flops=4 * blocks * size * size * cols, bytes_accessed=4 << 20, transcendentals=0
        ),
        name="add_far",
    )(offsets, counts, *far_tiles, arrived, *partials, queries)


def from_all(mine):
    count = lax.axis_size("pb")
    up = [(i, (i + 1) % count) for i in range(count)]
    down = [((i + 1) % count, i) for i in range(count)]
    across = [(i, (i + 2) % count) for i in range(count)]
    return [
        mine[0],
        lax.ppermute(mine[2], "pb", up),
        lax.ppermute(mine[1], "pb", down),
        lax.ppermute(mine[3], "pb", across),
    ]


def on_device(affinity_tiles, block_ids, valid_counts, queries):
    blocks, slots = block_ids.shape
    rows, size = affinity_tiles.shape[2:]
    cols = queries.shape[1]
    owners = lax.axis_size("db")
    first_block = lax.axis_index("db") * blocks
    far_tiles = from_all([affinity_tiles[:, FAR[0] : FAR[-1] + 1]] * 4)
    place = lax.axis_index("pb")
    offsets = jnp.stack([(place + shift) % lax.axis_size("pb") * rows for shift in (0, -1, 1, 2)])
    near_index = jnp.clip(block_ids - first_block + EDGE, 0, blocks + 2 * EDGE - 1)
    far = block_ids[:, FAR[0] : FAR[-1] + 1].reshape(1, -1)
    slots = far.shape[1]
    digits = jnp.concatenate([far // BASE, far % BASE], axis=1).astype(jnp.float32)
    digits = jnp.pad(digits, ((0, 0), (0, cols - 2 * slots)))
    up = [(i, i + 1) for i in range(owners - 1)]
    down = [(i + 1, i) for i in range(owners - 1)]
    ranking, wanted = queries, None
    pieces = split_blocks(queries, digits, blocks, size, owners)
    for step in range(ITERS):
        own = ranking.reshape(blocks, size, cols)
        low = lax.ppermute(own[blocks - EDGE :], "db", up)
        high = lax.ppermute(own[:EDGE], "db", down)
        panels = from_all([jnp.concatenate([low, own, high], axis=0)] * 4)
        held = lax.all_to_all(pieces, "db", split_axis=0, concat_axis=0, tiled=True)
        if wanted is None:
            chosen, wanted = select_pieces(held, slots, None, panels)
        else:
            (chosen,) = select_pieces(held, slots, wanted, panels)
        arrived = lax.all_to_all(
            chosen.reshape(owners, slots, -1), "db", split_axis=0, concat_axis=0, tiled=True
        ).reshape(chosen.shape)
        partials = from_all(near_product(near_index, valid_counts, affinity_tiles, panels))
        done = add_far(offsets, valid_counts, far_tiles, arrived, partials, queries, owners, step < ITERS - 1)
        ranking = done[0]
        pieces = done[-1]
    return ranking


def solution(mesh):
    return jax.shard_map(
        on_device,
        mesh=mesh,
        in_specs=(P("db", None, "pb", None), P("db", None), P("db"), P("db", "pb")),
        out_specs=P("db", "pb"),
        check_vma=False,
    )
```

```python
import jax
import jax.numpy as jnp
from jax import lax
from jax.experimental import pallas as pl
from jax.experimental.pallas import tpu as pltpu
from jax.sharding import PartitionSpec as P

EDGE = 2
ITERS = 2
BASE = 256
FAR = (1, 2)
LIMIT = 12 << 20
VMEM = pl.BlockSpec(memory_space=pltpu.VMEM)
SMEM = pl.BlockSpec(memory_space=pltpu.SMEM)


def rows_to_pieces(wide, pieces_ref, blocks, size, owners):
    for k in range(owners):
        for part in range(size // owners):
            rows = wide[pl.ds(part * owners + k, blocks, stride=size), :]
            pieces_ref[k, part * blocks : (part + 1) * blocks, :] = rows.astype(pieces_ref.dtype)


def split_blocks(queries, digits, blocks, size, owners):
    cols = queries.shape[1]
    rows = size // owners * blocks

    def kernel(q_ref, digits_ref, pieces_ref, wide):
        wide[...] = q_ref[...].astype(jnp.float32)
        rows_to_pieces(wide, pieces_ref, blocks, size, owners)
        for k in range(owners):
            pieces_ref[k, rows:, :] = jnp.broadcast_to(digits_ref[...], (8, cols)).astype(pieces_ref.dtype)

    return pl.pallas_call(
        kernel,
        out_shape=jax.ShapeDtypeStruct((owners, rows + 8, cols), queries.dtype),
        in_specs=[VMEM, VMEM],
        out_specs=VMEM,
        scratch_shapes=[pltpu.VMEM(queries.shape, jnp.float32)],
        name="split_blocks",
    )(queries, digits)


def select_pieces(held, slots, wanted=None):
    devices, height, cols = held.shape
    blocks = height // 16 * 8
    parts = 2
    block_total = devices * blocks
    group = 8

    def kernel(held_ref, *rest):
        if wanted is None:
            out_ref, wanted_out, flat = rest
            digits = held_ref[:, parts * blocks :, :].astype(jnp.float32)[:, 0, :].T
            ids = (digits[:slots] * BASE + digits[slots : 2 * slots]).astype(jnp.int32)
            wanted_out[...] = ids
        else:
            wanted_ref, out_ref, flat = rest
            ids = wanted_ref[...]
        for s in range(devices):
            for part in range(parts):
                flat[s * blocks : (s + 1) * blocks, part * cols : (part + 1) * cols] = held_ref[
                    s, part * blocks : (part + 1) * blocks, :
                ]
        column = lax.broadcasted_iota(jnp.int32, (slots, block_total), 1)
        for first in range(0, devices, group):
            hits = [
                jnp.where(
                    jnp.broadcast_to(ids[:, d : d + 1], (slots, block_total)) == column, 1.0, 0.0
                ).astype(held.dtype)
                for d in range(first, first + group)
            ]
            out_ref[first * slots : (first + group) * slots, :] = jnp.dot(
                jnp.concatenate(hits, axis=0), flat[...], preferred_element_type=jnp.float32
            ).astype(out_ref.dtype)

    out_shape = [jax.ShapeDtypeStruct((devices * slots, parts * cols), held.dtype)]
    if wanted is None:
        out_shape.append(jax.ShapeDtypeStruct((slots, devices), jnp.int32))
    operands = () if wanted is None else (wanted,)
    return pl.pallas_call(
        kernel,
        out_shape=out_shape,
        in_specs=[VMEM] * (1 + len(operands)),
        out_specs=[VMEM] * len(out_shape),
        scratch_shapes=[pltpu.VMEM((block_total, parts * cols), held.dtype)],
        compiler_params=pltpu.CompilerParams(vmem_limit_bytes=LIMIT),
        cost_estimate=pl.CostEstimate(
            flops=2 * devices * slots * block_total * parts * cols, bytes_accessed=2 << 20, transcendentals=0
        ),
        name="select_pieces",
    )(held, *operands)


def near_product(near_index, counts, places, tiles, own, edges):
    blocks, slots, rows, size = tiles.shape
    cols = own.shape[3]
    number = len(edges)
    group = 4
    near = [t for t in range(slots) if t not in FAR]

    def kernel(index_ref, count_ref, place_ref, tiles_ref, own_ref, *refs):
        edge_refs, out_refs, panels = refs[:number], refs[number : 2 * number], refs[2 * number]
        step = pl.program_id(0)

        @pl.when(step == 0)
        def _():
            for n in range(number):
                panels[n, :EDGE] = edge_refs[n][:EDGE]
                panels[n, EDGE : EDGE + blocks] = own_ref[place_ref[n]]
                panels[n, EDGE + blocks :] = edge_refs[n][EDGE:]

        for r in range(group):
            b = step * group + r
            total = jnp.zeros((rows, number * cols), jnp.float32)
            for first in range(0, len(near), 2):
                left, right = [], []
                for t in near[first : first + 2]:
                    tile = tiles_ref[r, t]
                    left.append(jnp.where(t < count_ref[b], tile, jnp.zeros_like(tile)))
                    right.append(jnp.concatenate([panels[n, index_ref[b, t]] for n in range(number)], axis=1))
                total += jnp.dot(
                    jnp.concatenate(left, axis=1),
                    jnp.concatenate(right, axis=0),
                    preferred_element_type=jnp.float32,
                )
            for n in range(number):
                out_refs[n][r] = total[:, n * cols : (n + 1) * cols]

    out_shape = jax.ShapeDtypeStruct((blocks, rows, cols), jnp.float32)
    return pl.pallas_call(
        kernel,
        out_shape=[out_shape] * number,
        grid_spec=pltpu.PrefetchScalarGridSpec(
            num_scalar_prefetch=3,
            grid=(blocks // group,),
            in_specs=[pl.BlockSpec((group, slots, rows, size), lambda i, *_: (i, 0, 0, 0))]
            + [VMEM] * (1 + number),
            out_specs=[pl.BlockSpec((group, rows, cols), lambda i, *_: (i, 0, 0))] * number,
            scratch_shapes=[pltpu.VMEM((number, blocks + 2 * EDGE, size, cols), own.dtype)],
        ),
        compiler_params=pltpu.CompilerParams(vmem_limit_bytes=LIMIT),
        cost_estimate=pl.CostEstimate(
            flops=2 * blocks * len(near) * number * rows * size * cols,
            bytes_accessed=6 << 20,
            transcendentals=0,
        ),
        name="near_product",
    )(near_index, counts, places, tiles, own, *edges)


def add_far(offsets, counts, far_tiles, arrived, partials, queries, owners, split):
    blocks, _, rows, size = far_tiles[0].shape
    cols = queries.shape[1]
    far = arrived.shape[0] // owners
    number = len(far_tiles)

    def kernel(offset_ref, count_ref, *refs):
        tiles = refs[:number]
        arrived_ref = refs[number]
        partial_refs = refs[number + 1 : number + 1 + len(partials)]
        q_ref, out_ref, *rest = refs[number + 1 + len(partials) :]
        if split:
            pieces_ref, upper, lower, wide = rest
        else:
            upper, lower = rest
        upper[...] = arrived_ref[:, :cols].astype(jnp.float32)
        lower[...] = arrived_ref[:, cols:].astype(jnp.float32)
        for b in range(blocks):
            left, right = [], []
            for s, t in enumerate(FAR):
                tile = jnp.concatenate([ref[b, s] for ref in tiles], axis=0)
                left.append(jnp.where(t < count_ref[b], tile, jnp.zeros_like(tile)))
                for half in (upper, lower):
                    right.append(half[pl.ds(2 * b + s, owners, stride=far), :].astype(queries.dtype))
            total = jnp.concatenate([ref[b] for ref in partial_refs], axis=0) + jnp.dot(
                jnp.concatenate(left, axis=1),
                jnp.concatenate(right, axis=0),
                preferred_element_type=jnp.float32,
            )
            for n in range(number):
                place = pl.ds(pl.multiple_of(b * size + offset_ref[n], rows), rows)
                result = 0.99 * total[n * rows : (n + 1) * rows] + q_ref[place, :].astype(jnp.float32)
                result = result.astype(out_ref.dtype)
                out_ref[place, :] = result
                if split:
                    wide[place, :] = result.astype(jnp.float32)
        if split:
            rows_to_pieces(wide, pieces_ref, blocks, size, owners)

    out_shape = [jax.ShapeDtypeStruct(queries.shape, queries.dtype)]
    out_specs = [pl.BlockSpec(queries.shape, lambda i, *_: (0, 0))]
    scratch = [pltpu.VMEM((owners * far, cols), jnp.float32)] * 2
    if split:
        shape = (owners, size // owners * blocks, cols)
        out_shape.append(jax.ShapeDtypeStruct(shape, queries.dtype))
        out_specs.append(pl.BlockSpec(shape, lambda i, *_: (0, 0, 0)))
        scratch.append(pltpu.VMEM(queries.shape, jnp.float32))
    return pl.pallas_call(
        kernel,
        out_shape=out_shape,
        grid_spec=pltpu.PrefetchScalarGridSpec(
            num_scalar_prefetch=2,
            grid=(1,),
            in_specs=[VMEM] * (number + 2 + len(partials)),
            out_specs=out_specs,
            scratch_shapes=scratch,
        ),
        compiler_params=pltpu.CompilerParams(vmem_limit_bytes=LIMIT),
        cost_estimate=pl.CostEstimate(
            flops=4 * blocks * size * size * cols, bytes_accessed=4 << 20, transcendentals=0
        ),
        name="add_far",
    )(offsets, counts, *far_tiles, arrived, *partials, queries)


def from_all(mine):
    count = lax.axis_size("pb")
    up = [(i, (i + 1) % count) for i in range(count)]
    down = [((i + 1) % count, i) for i in range(count)]
    across = [(i, (i + 2) % count) for i in range(count)]
    return [
        mine[0],
        lax.ppermute(mine[2], "pb", up),
        lax.ppermute(mine[1], "pb", down),
        lax.ppermute(mine[3], "pb", across),
    ]


def on_device(affinity_tiles, block_ids, valid_counts, queries):
    blocks, slots = block_ids.shape
    rows, size = affinity_tiles.shape[2:]
    cols = queries.shape[1]
    owners = lax.axis_size("db")
    first_block = lax.axis_index("db") * blocks
    far_tiles = from_all([affinity_tiles[:, FAR[0] : FAR[-1] + 1]] * 4)
    place = lax.axis_index("pb")
    places = jnp.stack([(place + shift) % lax.axis_size("pb") for shift in (0, -1, 1, 2)])
    offsets = places * rows
    near_index = jnp.clip(block_ids - first_block + EDGE, 0, blocks + 2 * EDGE - 1)
    far = block_ids[:, FAR[0] : FAR[-1] + 1].reshape(1, -1)
    slots = far.shape[1]
    digits = jnp.concatenate([far // BASE, far % BASE], axis=1).astype(jnp.float32)
    digits = jnp.pad(digits, ((0, 0), (0, cols - 2 * slots)))
    up = [(i, i + 1) for i in range(owners - 1)]
    down = [(i + 1, i) for i in range(owners - 1)]
    ranking, wanted = queries, None
    pieces = split_blocks(queries, digits, blocks, size, owners)
    for step in range(ITERS):
        own = ranking.reshape(blocks, size, cols)
        low = lax.ppermute(own[blocks - EDGE :], "db", up)
        high = lax.ppermute(own[:EDGE], "db", down)
        whole = lax.all_gather(own, "pb", axis=0)
        edges = from_all([jnp.concatenate([low, high], axis=0)] * 4)
        held = lax.all_to_all(pieces, "db", split_axis=0, concat_axis=0, tiled=True)
        if wanted is None:
            chosen, wanted = select_pieces(held, slots)
        else:
            (chosen,) = select_pieces(held, slots, wanted)
        arrived = lax.all_to_all(
            chosen.reshape(owners, slots, -1), "db", split_axis=0, concat_axis=0, tiled=True
        ).reshape(chosen.shape)
        partials = from_all(near_product(near_index, valid_counts, places, affinity_tiles, whole, edges))
        done = add_far(offsets, valid_counts, far_tiles, arrived, partials, queries, owners, step < ITERS - 1)
        ranking = done[0]
        pieces = done[-1]
    return ranking


def solution(mesh):
    return jax.shard_map(
        on_device,
        mesh=mesh,
        in_specs=(P("db", None, "pb", None), P("db", None), P("db"), P("db", "pb")),
        out_specs=P("db", "pb"),
        check_vma=False,
    )
```

```python
import jax
import jax.numpy as jnp
from jax import lax
from jax.experimental import pallas as pl
from jax.experimental.pallas import tpu as pltpu
from jax.sharding import PartitionSpec as P

EDGE = 2
ITERS = 2
BASE = 256
FAR = (1, 2)
LIMIT = 12 << 20
VMEM = pl.BlockSpec(memory_space=pltpu.VMEM)
HBM = pl.BlockSpec(memory_space=pltpu.HBM)


def in_hbm(arrays):
    return [pltpu.with_memory_space_constraint(array, pltpu.HBM) for array in arrays]


def rows_to_pieces(wide, pieces_ref, blocks, size, owners):
    for k in range(owners):
        for part in range(size // owners):
            rows = wide[pl.ds(part * owners + k, blocks, stride=size), :]
            pieces_ref[k, part * blocks : (part + 1) * blocks, :] = rows.astype(pieces_ref.dtype)


def split_blocks(queries, digits, blocks, size, owners):
    cols = queries.shape[1]
    rows = size // owners * blocks

    def kernel(q_ref, digits_ref, pieces_ref, wide):
        wide[...] = q_ref[...].astype(jnp.float32)
        rows_to_pieces(wide, pieces_ref, blocks, size, owners)
        for k in range(owners):
            pieces_ref[k, rows:, :] = jnp.broadcast_to(digits_ref[...], (8, cols)).astype(pieces_ref.dtype)

    return pl.pallas_call(
        kernel,
        out_shape=jax.ShapeDtypeStruct((owners, rows + 8, cols), queries.dtype),
        in_specs=[VMEM, VMEM],
        out_specs=VMEM,
        scratch_shapes=[pltpu.VMEM(queries.shape, jnp.float32)],
        name="split_blocks",
    )(queries, digits)


def select_pieces(held, slots, after, wanted=None):
    devices, height, cols = held.shape
    blocks = height // 16 * 8
    parts = 2
    block_total = devices * blocks
    group = 8

    def kernel(held_ref, *rest):
        rest = rest[len(after) :]
        if wanted is None:
            out_ref, wanted_out, flat = rest
            digits = held_ref[:, parts * blocks :, :].astype(jnp.float32)[:, 0, :].T
            ids = (digits[:slots] * BASE + digits[slots : 2 * slots]).astype(jnp.int32)
            wanted_out[...] = ids
        else:
            wanted_ref, out_ref, flat = rest
            ids = wanted_ref[...]
        for s in range(devices):
            for part in range(parts):
                flat[s * blocks : (s + 1) * blocks, part * cols : (part + 1) * cols] = held_ref[
                    s, part * blocks : (part + 1) * blocks, :
                ]
        column = lax.broadcasted_iota(jnp.int32, (slots, block_total), 1)
        for first in range(0, devices, group):
            hits = [
                jnp.where(
                    jnp.broadcast_to(ids[:, d : d + 1], (slots, block_total)) == column, 1.0, 0.0
                ).astype(held.dtype)
                for d in range(first, first + group)
            ]
            out_ref[first * slots : (first + group) * slots, :] = jnp.dot(
                jnp.concatenate(hits, axis=0), flat[...], preferred_element_type=jnp.float32
            ).astype(out_ref.dtype)

    out_shape = [jax.ShapeDtypeStruct((devices * slots, parts * cols), held.dtype)]
    if wanted is None:
        out_shape.append(jax.ShapeDtypeStruct((slots, devices), jnp.int32))
    operands = () if wanted is None else (wanted,)
    return pl.pallas_call(
        kernel,
        out_shape=out_shape,
        in_specs=[VMEM] + [HBM] * len(after) + [VMEM] * len(operands),
        out_specs=[VMEM] * len(out_shape),
        scratch_shapes=[pltpu.VMEM((block_total, parts * cols), held.dtype)],
        compiler_params=pltpu.CompilerParams(vmem_limit_bytes=LIMIT),
        cost_estimate=pl.CostEstimate(
            flops=2 * devices * slots * block_total * parts * cols, bytes_accessed=2 << 20, transcendentals=0
        ),
        name="select_pieces",
    )(held, *in_hbm(after), *operands)


def near_product(near_index, counts, places, tiles, own, edges):
    blocks, slots, rows, size = tiles.shape
    cols = own.shape[3]
    number = len(edges)
    group = 4
    near = [t for t in range(slots) if t not in FAR]

    def kernel(index_ref, count_ref, place_ref, tiles_ref, own_ref, *refs):
        edge_refs, out_refs = refs[:number], refs[number : 2 * number]
        panels, sems = refs[2 * number :]
        step = pl.program_id(0)

        @pl.when(step == 0)
        def _():
            copies = []
            for n in range(number):
                moves = (
                    (edge_refs[n].at[:EDGE], panels.at[n, :EDGE]),
                    (own_ref.at[place_ref[n]], panels.at[n, EDGE : EDGE + blocks]),
                    (edge_refs[n].at[EDGE:], panels.at[n, EDGE + blocks :]),
                )
                for m, (source, target) in enumerate(moves):
                    copies.append(pltpu.make_async_copy(source, target, sems.at[n, m]))
            for copy in copies:
                copy.start()
            for copy in copies:
                copy.wait()

        for r in range(group):
            b = step * group + r
            total = jnp.zeros((rows, number * cols), jnp.float32)
            for first in range(0, len(near), 2):
                left, right = [], []
                for t in near[first : first + 2]:
                    tile = tiles_ref[r, t]
                    left.append(jnp.where(t < count_ref[b], tile, jnp.zeros_like(tile)))
                    right.append(jnp.concatenate([panels[n, index_ref[b, t]] for n in range(number)], axis=1))
                total += jnp.dot(
                    jnp.concatenate(left, axis=1),
                    jnp.concatenate(right, axis=0),
                    preferred_element_type=jnp.float32,
                )
            for n in range(number):
                out_refs[n][r] = total[:, n * cols : (n + 1) * cols]

    out_shape = jax.ShapeDtypeStruct((blocks, rows, cols), jnp.float32)
    return pl.pallas_call(
        kernel,
        out_shape=[out_shape] * number,
        grid_spec=pltpu.PrefetchScalarGridSpec(
            num_scalar_prefetch=3,
            grid=(blocks // group,),
            in_specs=[pl.BlockSpec((group, slots, rows, size), lambda i, *_: (i, 0, 0, 0))]
            + [HBM] * (1 + number),
            out_specs=[pl.BlockSpec((group, rows, cols), lambda i, *_: (i, 0, 0))] * number,
            scratch_shapes=[
                pltpu.VMEM((number, blocks + 2 * EDGE, size, cols), own.dtype),
                pltpu.SemaphoreType.DMA((number, 3)),
            ],
        ),
        compiler_params=pltpu.CompilerParams(vmem_limit_bytes=LIMIT),
        cost_estimate=pl.CostEstimate(
            flops=2 * blocks * len(near) * number * rows * size * cols,
            bytes_accessed=6 << 20,
            transcendentals=0,
        ),
        name="near_product",
    )(near_index, counts, places, tiles, *in_hbm([own, *edges]))


def add_far(offsets, counts, far_tiles, arrived, partials, queries, owners, split):
    blocks, _, rows, size = far_tiles[0].shape
    cols = queries.shape[1]
    far = arrived.shape[0] // owners
    number = len(far_tiles)

    def kernel(offset_ref, count_ref, *refs):
        arrived_ref, q_ref, out_ref = refs[2 * number : 2 * number + 3]
        rest = refs[2 * number + 3 :]
        if split:
            pieces_ref, upper, lower, tiles, sums, sems, wide = rest
        else:
            upper, lower, tiles, sums, sems = rest
        copies = [
            pltpu.make_async_copy(refs[number * kind + n], target.at[n], sems.at[kind, n])
            for kind, target in enumerate((tiles, sums))
            for n in range(number)
        ]
        for copy in copies:
            copy.start()
        upper[...] = arrived_ref[:, :cols].astype(jnp.float32)
        lower[...] = arrived_ref[:, cols:].astype(jnp.float32)
        for copy in copies:
            copy.wait()
        for b in range(blocks):
            left, right = [], []
            for s, t in enumerate(FAR):
                tile = tiles[:, b, s].reshape(size, size)
                left.append(jnp.where(t < count_ref[b], tile, jnp.zeros_like(tile)))
                for half in (upper, lower):
                    right.append(half[pl.ds(2 * b + s, owners, stride=far), :].astype(queries.dtype))
            total = sums[:, b].reshape(size, cols) + jnp.dot(
                jnp.concatenate(left, axis=1),
                jnp.concatenate(right, axis=0),
                preferred_element_type=jnp.float32,
            )
            for n in range(number):
                place = pl.ds(pl.multiple_of(b * size + offset_ref[n], rows), rows)
                result = 0.99 * total[n * rows : (n + 1) * rows] + q_ref[place, :].astype(jnp.float32)
                result = result.astype(out_ref.dtype)
                out_ref[place, :] = result
                if split:
                    wide[place, :] = result.astype(jnp.float32)
        if split:
            rows_to_pieces(wide, pieces_ref, blocks, size, owners)

    out_shape = [jax.ShapeDtypeStruct(queries.shape, queries.dtype)]
    out_specs = [pl.BlockSpec(queries.shape, lambda i, *_: (0, 0))]
    scratch = [
        pltpu.VMEM((owners * far, cols), jnp.float32),
        pltpu.VMEM((owners * far, cols), jnp.float32),
        pltpu.VMEM((number,) + far_tiles[0].shape, far_tiles[0].dtype),
        pltpu.VMEM((number,) + partials[0].shape, partials[0].dtype),
        pltpu.SemaphoreType.DMA((2, number)),
    ]
    if split:
        shape = (owners, size // owners * blocks, cols)
        out_shape.append(jax.ShapeDtypeStruct(shape, queries.dtype))
        out_specs.append(pl.BlockSpec(shape, lambda i, *_: (0, 0, 0)))
        scratch.append(pltpu.VMEM(queries.shape, jnp.float32))
    return pl.pallas_call(
        kernel,
        out_shape=out_shape,
        grid_spec=pltpu.PrefetchScalarGridSpec(
            num_scalar_prefetch=2,
            grid=(1,),
            in_specs=[HBM] * (2 * number) + [VMEM] * 2,
            out_specs=out_specs,
            scratch_shapes=scratch,
        ),
        compiler_params=pltpu.CompilerParams(vmem_limit_bytes=LIMIT),
        cost_estimate=pl.CostEstimate(
            flops=4 * blocks * size * size * cols, bytes_accessed=4 << 20, transcendentals=0
        ),
        name="add_far",
    )(offsets, counts, *in_hbm(far_tiles), *in_hbm(partials), arrived, queries)


def from_all(mine):
    count = lax.axis_size("pb")
    up = [(i, (i + 1) % count) for i in range(count)]
    down = [((i + 1) % count, i) for i in range(count)]
    across = [(i, (i + 2) % count) for i in range(count)]
    return [
        mine[0],
        lax.ppermute(mine[2], "pb", up),
        lax.ppermute(mine[1], "pb", down),
        lax.ppermute(mine[3], "pb", across),
    ]


def on_device(affinity_tiles, block_ids, valid_counts, queries):
    blocks, slots = block_ids.shape
    rows, size = affinity_tiles.shape[2:]
    cols = queries.shape[1]
    owners = lax.axis_size("db")
    first_block = lax.axis_index("db") * blocks
    far_tiles = from_all([affinity_tiles[:, FAR[0] : FAR[-1] + 1]] * 4)
    place = lax.axis_index("pb")
    places = jnp.stack([(place + shift) % lax.axis_size("pb") for shift in (0, -1, 1, 2)])
    offsets = places * rows
    near_index = jnp.clip(block_ids - first_block + EDGE, 0, blocks + 2 * EDGE - 1)
    far = block_ids[:, FAR[0] : FAR[-1] + 1].reshape(1, -1)
    slots = far.shape[1]
    digits = jnp.concatenate([far // BASE, far % BASE], axis=1).astype(jnp.float32)
    digits = jnp.pad(digits, ((0, 0), (0, cols - 2 * slots)))
    up = [(i, i + 1) for i in range(owners - 1)]
    down = [(i + 1, i) for i in range(owners - 1)]
    ranking, wanted = queries, None
    pieces = split_blocks(queries, digits, blocks, size, owners)
    for step in range(ITERS):
        own = ranking.reshape(blocks, size, cols)
        low = lax.ppermute(own[blocks - EDGE :], "db", up)
        high = lax.ppermute(own[:EDGE], "db", down)
        whole = lax.all_gather(own, "pb", axis=0)
        edges = from_all([jnp.concatenate([low, high], axis=0)] * 4)
        held = lax.all_to_all(pieces, "db", split_axis=0, concat_axis=0, tiled=True)
        if wanted is None:
            chosen, wanted = select_pieces(held, slots, edges)
        else:
            (chosen,) = select_pieces(held, slots, edges, wanted)
        arrived = lax.all_to_all(
            chosen.reshape(owners, slots, -1), "db", split_axis=0, concat_axis=0, tiled=True
        ).reshape(chosen.shape)
        partials = from_all(near_product(near_index, valid_counts, places, affinity_tiles, whole, edges))
        done = add_far(offsets, valid_counts, far_tiles, arrived, partials, queries, owners, step < ITERS - 1)
        ranking = done[0]
        pieces = done[-1]
    return ranking


def solution(mesh):
    return jax.shard_map(
        on_device,
        mesh=mesh,
        in_specs=(P("db", None, "pb", None), P("db", None), P("db"), P("db", "pb")),
        out_specs=P("db", "pb"),
        check_vma=False,
    )
```

```python
import jax
import jax.numpy as jnp
from jax import lax
from jax.experimental import pallas as pl
from jax.experimental.pallas import tpu as pltpu
from jax.sharding import PartitionSpec as P

EDGE = 2
ITERS = 2
BASE = 256
FAR = (1, 2)
LIMIT = 12 << 20
VMEM = pl.BlockSpec(memory_space=pltpu.VMEM)
HBM = pl.BlockSpec(memory_space=pltpu.HBM)


def in_hbm(arrays):
    return [pltpu.with_memory_space_constraint(array, pltpu.HBM) for array in arrays]


def rows_to_pieces(wide, pieces_ref, blocks, size, owners):
    for k in range(owners):
        for part in range(size // owners):
            rows = wide[pl.ds(part * owners + k, blocks, stride=size), :]
            pieces_ref[k, part * blocks : (part + 1) * blocks, :] = rows.astype(pieces_ref.dtype)


def split_blocks(queries, digits, blocks, size, owners):
    cols = queries.shape[1]
    rows = size // owners * blocks

    def kernel(q_ref, digits_ref, pieces_ref, wide):
        wide[...] = q_ref[...].astype(jnp.float32)
        rows_to_pieces(wide, pieces_ref, blocks, size, owners)
        for k in range(owners):
            pieces_ref[k, rows:, :] = jnp.broadcast_to(digits_ref[...], (8, cols)).astype(pieces_ref.dtype)

    return pl.pallas_call(
        kernel,
        out_shape=jax.ShapeDtypeStruct((owners, rows + 8, cols), queries.dtype),
        in_specs=[VMEM, VMEM],
        out_specs=VMEM,
        scratch_shapes=[pltpu.VMEM(queries.shape, jnp.float32)],
        name="split_blocks",
    )(queries, digits)


def select_pieces(held, slots, after, wanted=None):
    devices, height, cols = held.shape
    blocks = height // 16 * 8
    parts = 2
    block_total = devices * blocks
    group = 8

    def kernel(held_ref, *rest):
        rest = rest[len(after) :]
        if wanted is None:
            out_ref, wanted_out, flat = rest
            digits = held_ref[:, parts * blocks :, :].astype(jnp.float32)[:, 0, :].T
            ids = (digits[:slots] * BASE + digits[slots : 2 * slots]).astype(jnp.int32)
            wanted_out[...] = ids
        else:
            wanted_ref, out_ref, flat = rest
            ids = wanted_ref[...]
        for s in range(devices):
            for part in range(parts):
                flat[s * blocks : (s + 1) * blocks, part * cols : (part + 1) * cols] = held_ref[
                    s, part * blocks : (part + 1) * blocks, :
                ]
        column = lax.broadcasted_iota(jnp.int32, (slots, block_total), 1)
        for first in range(0, devices, group):
            hits = [
                jnp.where(
                    jnp.broadcast_to(ids[:, d : d + 1], (slots, block_total)) == column, 1.0, 0.0
                ).astype(held.dtype)
                for d in range(first, first + group)
            ]
            out_ref[first * slots : (first + group) * slots, :] = jnp.dot(
                jnp.concatenate(hits, axis=0), flat[...], preferred_element_type=jnp.float32
            ).astype(out_ref.dtype)

    out_shape = [jax.ShapeDtypeStruct((devices * slots, parts * cols), held.dtype)]
    if wanted is None:
        out_shape.append(jax.ShapeDtypeStruct((slots, devices), jnp.int32))
    operands = () if wanted is None else (wanted,)
    return pl.pallas_call(
        kernel,
        out_shape=out_shape,
        in_specs=[VMEM] + [HBM] * len(after) + [VMEM] * len(operands),
        out_specs=[VMEM] * len(out_shape),
        scratch_shapes=[pltpu.VMEM((block_total, parts * cols), held.dtype)],
        compiler_params=pltpu.CompilerParams(vmem_limit_bytes=LIMIT),
        cost_estimate=pl.CostEstimate(
            flops=2 * devices * slots * block_total * parts * cols, bytes_accessed=2 << 20, transcendentals=0
        ),
        name="select_pieces",
    )(held, *in_hbm(after), *operands)


def near_product(near_index, counts, tiles, own, edges):
    blocks, slots, rows, size = tiles.shape
    cols = own[0].shape[2]
    number = len(own)
    group = 4
    near = [t for t in range(slots) if t not in FAR]

    def kernel(index_ref, count_ref, tiles_ref, *refs):
        own_refs, edge_refs, out_refs = [refs[k * number : (k + 1) * number] for k in range(3)]
        panels, sems = refs[3 * number :]
        step = pl.program_id(0)

        @pl.when(step == 0)
        def _():
            copies = []
            for n in range(number):
                moves = (
                    (edge_refs[n].at[:EDGE], panels.at[n, :EDGE]),
                    (own_refs[n], panels.at[n, EDGE : EDGE + blocks]),
                    (edge_refs[n].at[EDGE:], panels.at[n, EDGE + blocks :]),
                )
                for m, (source, target) in enumerate(moves):
                    copies.append(pltpu.make_async_copy(source, target, sems.at[n, m]))
            for copy in copies:
                copy.start()
            for copy in copies:
                copy.wait()

        for r in range(group):
            b = step * group + r
            total = jnp.zeros((rows, number * cols), jnp.float32)
            for first in range(0, len(near), 2):
                left, right = [], []
                for t in near[first : first + 2]:
                    tile = tiles_ref[r, t]
                    left.append(jnp.where(t < count_ref[b], tile, jnp.zeros_like(tile)))
                    right.append(jnp.concatenate([panels[n, index_ref[b, t]] for n in range(number)], axis=1))
                total += jnp.dot(
                    jnp.concatenate(left, axis=1),
                    jnp.concatenate(right, axis=0),
                    preferred_element_type=jnp.float32,
                )
            for n in range(number):
                out_refs[n][r] = total[:, n * cols : (n + 1) * cols]

    out_shape = jax.ShapeDtypeStruct((blocks, rows, cols), jnp.float32)
    return pl.pallas_call(
        kernel,
        out_shape=[out_shape] * number,
        grid_spec=pltpu.PrefetchScalarGridSpec(
            num_scalar_prefetch=2,
            grid=(blocks // group,),
            in_specs=[pl.BlockSpec((group, slots, rows, size), lambda i, *_: (i, 0, 0, 0))]
            + [HBM] * (2 * number),
            out_specs=[pl.BlockSpec((group, rows, cols), lambda i, *_: (i, 0, 0))] * number,
            scratch_shapes=[
                pltpu.VMEM((number, blocks + 2 * EDGE, size, cols), own[0].dtype),
                pltpu.SemaphoreType.DMA((number, 3)),
            ],
        ),
        compiler_params=pltpu.CompilerParams(vmem_limit_bytes=LIMIT),
        cost_estimate=pl.CostEstimate(
            flops=2 * blocks * len(near) * number * rows * size * cols,
            bytes_accessed=6 << 20,
            transcendentals=0,
        ),
        name="near_product",
    )(near_index, counts, tiles, *in_hbm([*own, *edges]))


def add_far(offsets, counts, far_tiles, arrived, partials, queries, owners, split):
    blocks, _, rows, size = far_tiles[0].shape
    cols = queries.shape[1]
    far = arrived.shape[0] // owners
    number = len(far_tiles)

    def kernel(offset_ref, count_ref, *refs):
        arrived_ref, q_ref, out_ref = refs[2 * number : 2 * number + 3]
        rest = refs[2 * number + 3 :]
        if split:
            pieces_ref, upper, lower, tiles, sums, sems, wide = rest
        else:
            upper, lower, tiles, sums, sems = rest
        copies = [
            pltpu.make_async_copy(refs[number * kind + n], target.at[n], sems.at[kind, n])
            for kind, target in enumerate((tiles, sums))
            for n in range(number)
        ]
        for copy in copies:
            copy.start()
        upper[...] = arrived_ref[:, :cols].astype(jnp.float32)
        lower[...] = arrived_ref[:, cols:].astype(jnp.float32)
        for copy in copies:
            copy.wait()
        for b in range(blocks):
            left, right = [], []
            for s, t in enumerate(FAR):
                tile = tiles[:, b, s].reshape(size, size)
                left.append(jnp.where(t < count_ref[b], tile, jnp.zeros_like(tile)))
                for half in (upper, lower):
                    right.append(half[pl.ds(2 * b + s, owners, stride=far), :].astype(queries.dtype))
            total = sums[:, b].reshape(size, cols) + jnp.dot(
                jnp.concatenate(left, axis=1),
                jnp.concatenate(right, axis=0),
                preferred_element_type=jnp.float32,
            )
            for n in range(number):
                place = pl.ds(pl.multiple_of(b * size + offset_ref[n], rows), rows)
                result = 0.99 * total[n * rows : (n + 1) * rows] + q_ref[place, :].astype(jnp.float32)
                result = result.astype(out_ref.dtype)
                out_ref[place, :] = result
                if split:
                    wide[place, :] = result.astype(jnp.float32)
        if split:
            rows_to_pieces(wide, pieces_ref, blocks, size, owners)

    out_shape = [jax.ShapeDtypeStruct(queries.shape, queries.dtype)]
    out_specs = [pl.BlockSpec(queries.shape, lambda i, *_: (0, 0))]
    scratch = [
        pltpu.VMEM((owners * far, cols), jnp.float32),
        pltpu.VMEM((owners * far, cols), jnp.float32),
        pltpu.VMEM((number,) + far_tiles[0].shape, far_tiles[0].dtype),
        pltpu.VMEM((number,) + partials[0].shape, partials[0].dtype),
        pltpu.SemaphoreType.DMA((2, number)),
    ]
    if split:
        shape = (owners, size // owners * blocks, cols)
        out_shape.append(jax.ShapeDtypeStruct(shape, queries.dtype))
        out_specs.append(pl.BlockSpec(shape, lambda i, *_: (0, 0, 0)))
        scratch.append(pltpu.VMEM(queries.shape, jnp.float32))
    return pl.pallas_call(
        kernel,
        out_shape=out_shape,
        grid_spec=pltpu.PrefetchScalarGridSpec(
            num_scalar_prefetch=2,
            grid=(1,),
            in_specs=[HBM] * (2 * number) + [VMEM] * 2,
            out_specs=out_specs,
            scratch_shapes=scratch,
        ),
        compiler_params=pltpu.CompilerParams(vmem_limit_bytes=LIMIT),
        cost_estimate=pl.CostEstimate(
            flops=4 * blocks * size * size * cols, bytes_accessed=4 << 20, transcendentals=0
        ),
        name="add_far",
    )(offsets, counts, *in_hbm(far_tiles), *in_hbm(partials), arrived, queries)


def from_all(mine):
    count = lax.axis_size("pb")
    up = [(i, (i + 1) % count) for i in range(count)]
    down = [((i + 1) % count, i) for i in range(count)]
    across = [(i, (i + 2) % count) for i in range(count)]
    return [
        mine[0],
        lax.ppermute(mine[2], "pb", up),
        lax.ppermute(mine[1], "pb", down),
        lax.ppermute(mine[3], "pb", across),
    ]


def on_device(affinity_tiles, block_ids, valid_counts, queries):
    blocks, slots = block_ids.shape
    rows, size = affinity_tiles.shape[2:]
    cols = queries.shape[1]
    owners = lax.axis_size("db")
    first_block = lax.axis_index("db") * blocks
    far_tiles = from_all([affinity_tiles[:, FAR[0] : FAR[-1] + 1]] * 4)
    place = lax.axis_index("pb")
    offsets = jnp.stack([(place + shift) % lax.axis_size("pb") * rows for shift in (0, -1, 1, 2)])
    near_index = jnp.clip(block_ids - first_block + EDGE, 0, blocks + 2 * EDGE - 1)
    far = block_ids[:, FAR[0] : FAR[-1] + 1].reshape(1, -1)
    slots = far.shape[1]
    digits = jnp.concatenate([far // BASE, far % BASE], axis=1).astype(jnp.float32)
    digits = jnp.pad(digits, ((0, 0), (0, cols - 2 * slots)))
    up = [(i, i + 1) for i in range(owners - 1)]
    down = [(i + 1, i) for i in range(owners - 1)]
    ranking, wanted = queries, None
    pieces = split_blocks(queries, digits, blocks, size, owners)
    for step in range(ITERS):
        own = ranking.reshape(blocks, size, cols)
        low = lax.ppermute(own[blocks - EDGE :], "db", up)
        high = lax.ppermute(own[:EDGE], "db", down)
        pieces, low, high = lax.optimization_barrier((pieces, low, high))
        held = lax.all_to_all(pieces, "db", split_axis=0, concat_axis=0, tiled=True)
        edges = from_all([jnp.concatenate([low, high], axis=0)] * 4)
        panels = from_all([own] * 4)
        after = edges + panels[1:3]
        if wanted is None:
            chosen, wanted = select_pieces(held, slots, after)
        else:
            (chosen,) = select_pieces(held, slots, after, wanted)
        arrived = lax.all_to_all(
            chosen.reshape(owners, slots, -1), "db", split_axis=0, concat_axis=0, tiled=True
        ).reshape(chosen.shape)
        products = list(near_product(near_index, valid_counts, affinity_tiles, panels[:3], edges[:3]))
        products[0], opposite = lax.optimization_barrier((products[0], panels[3]))
        products += near_product(near_index, valid_counts, affinity_tiles, [opposite], edges[3:])
        partials = from_all(products)
        done = add_far(offsets, valid_counts, far_tiles, arrived, partials, queries, owners, step < ITERS - 1)
        ranking = done[0]
        pieces = done[-1]
    return ranking


def solution(mesh):
    return jax.shard_map(
        on_device,
        mesh=mesh,
        in_specs=(P("db", None, "pb", None), P("db", None), P("db"), P("db", "pb")),
        out_specs=P("db", "pb"),
        check_vma=False,
    )
```

```python
import jax
import jax.numpy as jnp
from jax import lax
from jax.experimental import pallas as pl
from jax.experimental.pallas import tpu as pltpu
from jax.sharding import PartitionSpec as P

EDGE = 2
ITERS = 2
BASE = 256
FAR = (1, 2)
LOW = tuple(range(1, 9))
HIGH = tuple(range(9, 16)) + (0,)
VMEM = pl.BlockSpec(memory_space=pltpu.VMEM)
HBM = pl.BlockSpec(memory_space=pltpu.HBM)
LIMIT = 12 << 20


def in_hbm(arrays):
    return [pltpu.with_memory_space_constraint(array, pltpu.HBM) for array in arrays]


def rows_to_pieces(wide, pieces_ref, blocks, size, owners):
    for k in range(owners):
        for part in range(size // owners):
            rows = wide[pl.ds(part * owners + k, blocks, stride=size), :]
            pieces_ref[k, part * blocks : (part + 1) * blocks, :] = rows.astype(pieces_ref.dtype)


def split_blocks(queries, digits, blocks, size, owners):
    cols = queries.shape[1]
    rows = size // owners * blocks

    def kernel(q_ref, digits_ref, pieces_ref, wide):
        wide[...] = q_ref[...].astype(jnp.float32)
        rows_to_pieces(wide, pieces_ref, blocks, size, owners)
        for k in range(owners):
            pieces_ref[k, rows:, :] = jnp.broadcast_to(digits_ref[...], (8, cols)).astype(pieces_ref.dtype)

    return pl.pallas_call(
        kernel,
        out_shape=jax.ShapeDtypeStruct((owners, rows + 8, cols), queries.dtype),
        in_specs=[VMEM, VMEM],
        out_specs=VMEM,
        scratch_shapes=[pltpu.VMEM(queries.shape, jnp.float32)],
        name="split_blocks",
    )(queries, digits)


def select_pieces(held, slots, after, wanted=None):
    devices, height, cols = held.shape
    blocks = height // 16 * 8
    parts = 2
    block_total = devices * blocks
    group = 8

    def kernel(held_ref, *rest):
        rest = rest[len(after) :]
        if wanted is None:
            out_ref, wanted_out, flat = rest
            digits = held_ref[:, parts * blocks :, :].astype(jnp.float32)[:, 0, :].T
            ids = (digits[:slots] * BASE + digits[slots : 2 * slots]).astype(jnp.int32)
            wanted_out[...] = ids
        else:
            wanted_ref, out_ref, flat = rest
            ids = wanted_ref[...]
        for s in range(devices):
            for part in range(parts):
                flat[s * blocks : (s + 1) * blocks, part * cols : (part + 1) * cols] = held_ref[
                    s, part * blocks : (part + 1) * blocks, :
                ]
        column = lax.broadcasted_iota(jnp.int32, (slots, block_total), 1)
        for first in range(0, devices, group):
            hits = [
                jnp.where(
                    jnp.broadcast_to(ids[:, d : d + 1], (slots, block_total)) == column, 1.0, 0.0
                ).astype(held.dtype)
                for d in range(first, first + group)
            ]
            out_ref[first * slots : (first + group) * slots, :] = jnp.dot(
                jnp.concatenate(hits, axis=0), flat[...], preferred_element_type=jnp.float32
            ).astype(out_ref.dtype)

    out_shape = [jax.ShapeDtypeStruct((devices * slots, parts * cols), held.dtype)]
    if wanted is None:
        out_shape.append(jax.ShapeDtypeStruct((slots, devices), jnp.int32))
    operands = () if wanted is None else (wanted,)
    return pl.pallas_call(
        kernel,
        out_shape=out_shape,
        in_specs=[VMEM] + [HBM] * len(after) + [VMEM] * len(operands),
        out_specs=[VMEM] * len(out_shape),
        scratch_shapes=[pltpu.VMEM((block_total, parts * cols), held.dtype)],
        compiler_params=pltpu.CompilerParams(vmem_limit_bytes=LIMIT),
        cost_estimate=pl.CostEstimate(
            flops=2 * devices * slots * block_total * parts * cols, bytes_accessed=2 << 20, transcendentals=0
        ),
        name="select_pieces",
    )(held, *in_hbm(after), *operands)


def near_product(near_index, counts, quarters, low, own, high):
    blocks, _, rows, size = quarters[0][0].shape
    cols = own.shape[2]
    group = 4
    number = len(quarters)
    near = [(half, place, t) for half, names in enumerate((LOW, HIGH)) for place, t in enumerate(names)]
    near = [entry for entry in near if entry[2] not in FAR]

    def kernel(index_ref, count_ref, *refs):
        tiles = [refs[2 * n : 2 * n + 2] for n in range(number)]
        low_ref, own_ref, high_ref, out_ref, panels, sems = refs[2 * number :]
        step = pl.program_id(0)

        @pl.when(step == 0)
        def _():
            copies = [
                pltpu.make_async_copy(low_ref, panels.at[:EDGE], sems.at[0]),
                pltpu.make_async_copy(own_ref, panels.at[EDGE : EDGE + blocks], sems.at[1]),
                pltpu.make_async_copy(high_ref, panels.at[EDGE + blocks :], sems.at[2]),
            ]
            for copy in copies:
                copy.start()
            for copy in copies:
                copy.wait()

        for r in range(group):
            b = step * group + r
            total = jnp.zeros((number * rows, cols), jnp.float32)
            for first in range(0, len(near), 2):
                left, right = [], []
                for half, place, t in near[first : first + 2]:
                    tile = jnp.concatenate([pair[half][r, place] for pair in tiles], axis=0)
                    left.append(jnp.where(t < count_ref[b], tile, jnp.zeros_like(tile)))
                    right.append(panels[index_ref[b, t]])
                total += jnp.dot(
                    jnp.concatenate(left, axis=1),
                    jnp.concatenate(right, axis=0),
                    preferred_element_type=jnp.float32,
                )
            out_ref[r] = total

    return pl.pallas_call(
        kernel,
        out_shape=jax.ShapeDtypeStruct((blocks, number * rows, cols), jnp.float32),
        grid_spec=pltpu.PrefetchScalarGridSpec(
            num_scalar_prefetch=2,
            grid=(blocks // group,),
            in_specs=[
                pl.BlockSpec((group, half.shape[1], rows, size), lambda i, *_: (i, 0, 0, 0))
                for pair in quarters
                for half in pair
            ]
            + [HBM] * 3,
            out_specs=pl.BlockSpec((group, number * rows, cols), lambda i, *_: (i, 0, 0)),
            scratch_shapes=[
                pltpu.VMEM((blocks + 2 * EDGE, size, cols), own.dtype),
                pltpu.SemaphoreType.DMA((3,)),
            ],
        ),
        compiler_params=pltpu.CompilerParams(vmem_limit_bytes=LIMIT),
        cost_estimate=pl.CostEstimate(
            flops=2 * blocks * len(near) * number * rows * size * cols,
            bytes_accessed=number << 21,
            transcendentals=0,
        ),
        name="near_product",
    )(near_index, counts, *[half for pair in quarters for half in pair], *in_hbm([low, own, high]))


def add_far(offsets, counts, far_tiles, arrived, partials, queries, owners, split):
    blocks, _, rows, size = far_tiles[0].shape
    cols = queries.shape[1]
    far = arrived.shape[0] // owners
    number = len(far_tiles)

    def kernel(offset_ref, count_ref, *refs):
        tile_refs, partial_refs = refs[:number], refs[number : number + len(partials)]
        arrived_ref, q_ref, out_ref = refs[number + len(partials) : number + len(partials) + 3]
        rest = refs[number + len(partials) + 3 :]
        if split:
            pieces_ref, upper, lower, tiles, sums, sems, wide = rest
        else:
            upper, lower, tiles, sums, sems = rest
        copies = [
            pltpu.make_async_copy(ref.at[:, : len(FAR)], tiles.at[n], sems.at[0, n])
            for n, ref in enumerate(tile_refs)
        ]
        first = 0
        for n, (ref, part) in enumerate(zip(partial_refs, partials)):
            copies.append(
                pltpu.make_async_copy(ref, sums.at[:, first : first + part.shape[1]], sems.at[1, n])
            )
            first += part.shape[1]
        for copy in copies:
            copy.start()
        upper[...] = arrived_ref[:, :cols].astype(jnp.float32)
        lower[...] = arrived_ref[:, cols:].astype(jnp.float32)
        for copy in copies:
            copy.wait()
        for b in range(blocks):
            left, right = [], []
            for s, t in enumerate(FAR):
                tile = tiles[:, b, s].reshape(size, size)
                left.append(jnp.where(t < count_ref[b], tile, jnp.zeros_like(tile)))
                for half in (upper, lower):
                    right.append(half[pl.ds(2 * b + s, owners, stride=far), :].astype(queries.dtype))
            total = sums[b] + jnp.dot(
                jnp.concatenate(left, axis=1),
                jnp.concatenate(right, axis=0),
                preferred_element_type=jnp.float32,
            )
            for n in range(number):
                place = pl.ds(pl.multiple_of(b * size + offset_ref[n], rows), rows)
                result = 0.99 * total[n * rows : (n + 1) * rows] + q_ref[place, :].astype(jnp.float32)
                result = result.astype(out_ref.dtype)
                out_ref[place, :] = result
                if split:
                    wide[place, :] = result.astype(jnp.float32)
        if split:
            rows_to_pieces(wide, pieces_ref, blocks, size, owners)

    out_shape = [jax.ShapeDtypeStruct(queries.shape, queries.dtype)]
    out_specs = [pl.BlockSpec(queries.shape, lambda i, *_: (0, 0))]
    scratch = [
        pltpu.VMEM((owners * far, cols), jnp.float32),
        pltpu.VMEM((owners * far, cols), jnp.float32),
        pltpu.VMEM((number, blocks, len(FAR), rows, size), far_tiles[0].dtype),
        pltpu.VMEM((blocks, size, cols), jnp.float32),
        pltpu.SemaphoreType.DMA((2, number)),
    ]
    if split:
        shape = (owners, size // owners * blocks, cols)
        out_shape.append(jax.ShapeDtypeStruct(shape, queries.dtype))
        out_specs.append(pl.BlockSpec(shape, lambda i, *_: (0, 0, 0)))
        scratch.append(pltpu.VMEM(queries.shape, jnp.float32))
    return pl.pallas_call(
        kernel,
        out_shape=out_shape,
        grid_spec=pltpu.PrefetchScalarGridSpec(
            num_scalar_prefetch=2,
            grid=(1,),
            in_specs=[HBM] * (number + len(partials)) + [VMEM] * 2,
            out_specs=out_specs,
            scratch_shapes=scratch,
        ),
        compiler_params=pltpu.CompilerParams(vmem_limit_bytes=LIMIT),
        cost_estimate=pl.CostEstimate(
            flops=4 * blocks * size * size * cols, bytes_accessed=4 << 20, transcendentals=0
        ),
        name="add_far",
    )(offsets, counts, *in_hbm(far_tiles), *in_hbm(partials), arrived, queries)


def gather_rows(tiles):
    count = lax.axis_size("pb")
    up = [(i, (i + 1) % count) for i in range(count)]
    down = [((i + 1) % count, i) for i in range(count)]
    low = tiles[:, LOW[0] : LOW[-1] + 1]
    high = jnp.concatenate([tiles[:, HIGH[0] :], tiles[:, :1]], axis=1)
    before_low = lax.ppermute(low, "pb", up)
    after_high = lax.ppermute(high, "pb", down)
    before_high = lax.ppermute(high, "pb", up)
    after_low = lax.ppermute(low, "pb", down)
    far_low = lax.ppermute(before_low, "pb", up)
    far_high = lax.ppermute(after_high, "pb", down)
    return [(low, high), (before_low, before_high), (after_low, after_high), (far_low, far_high)]


def on_device(affinity_tiles, block_ids, valid_counts, queries):
    blocks, slots = block_ids.shape
    rows, size = affinity_tiles.shape[2:]
    cols = queries.shape[1]
    owners = lax.axis_size("db")
    first_block = lax.axis_index("db") * blocks
    quarters = gather_rows(affinity_tiles)
    far_tiles = [pair[0] for pair in quarters]
    place = lax.axis_index("pb")
    offsets = jnp.stack([(place + shift) % lax.axis_size("pb") * rows for shift in (0, -1, 1, 2)])
    near_index = jnp.clip(block_ids - first_block + EDGE, 0, blocks + 2 * EDGE - 1)
    far = block_ids[:, FAR[0] : FAR[-1] + 1].reshape(1, -1)
    slots = far.shape[1]
    digits = jnp.concatenate([far // BASE, far % BASE], axis=1).astype(jnp.float32)
    digits = jnp.pad(digits, ((0, 0), (0, cols - 2 * slots)))
    up = [(i, i + 1) for i in range(owners - 1)]
    down = [(i + 1, i) for i in range(owners - 1)]
    ranking, wanted = queries, None
    pieces = split_blocks(queries, digits, blocks, size, owners)
    for step in range(ITERS):
        own = ranking.reshape(blocks, size, cols)
        held = lax.all_to_all(pieces, "db", split_axis=0, concat_axis=0, tiled=True)
        low = lax.ppermute(own[blocks - EDGE :], "db", up)
        high = lax.ppermute(own[:EDGE], "db", down)
        if wanted is None:
            chosen, wanted = select_pieces(held, slots, [low, high])
        else:
            (chosen,) = select_pieces(held, slots, [low, high], wanted)
        arrived = lax.all_to_all(
            chosen.reshape(owners, slots, -1), "db", split_axis=0, concat_axis=0, tiled=True
        ).reshape(chosen.shape)
        partials = [
            near_product(near_index, valid_counts, part, low, own, high)
            for part in ([quarters[:3], quarters[3:]] if step == 0 else [quarters])
        ]
        done = add_far(offsets, valid_counts, far_tiles, arrived, partials, queries, owners, step < ITERS - 1)
        ranking = done[0]
        pieces = done[-1]
    return ranking


def solution(mesh):
    return jax.shard_map(
        on_device,
        mesh=mesh,
        in_specs=(P("db", None, "pb", None), P("db", None), P("db"), P("db", "pb")),
        out_specs=P("db", "pb"),
        check_vma=False,
    )
```

```python
import jax
import jax.numpy as jnp
from jax import lax
from jax.experimental import pallas as pl
from jax.experimental.pallas import tpu as pltpu
from jax.sharding import PartitionSpec as P

EDGE = 2
ITERS = 2
BASE = 256
FAR = (1, 2)
VMEM = pl.BlockSpec(memory_space=pltpu.VMEM)
HBM = pl.BlockSpec(memory_space=pltpu.HBM)
LIMIT = 12 << 20


def in_hbm(arrays):
    return [pltpu.with_memory_space_constraint(array, pltpu.HBM) for array in arrays]


def rows_to_pieces(wide, pieces_ref, blocks, size, owners):
    for k in range(owners):
        for part in range(size // owners):
            rows = wide[pl.ds(part * owners + k, blocks, stride=size), :]
            pieces_ref[k, part * blocks : (part + 1) * blocks, :] = rows.astype(pieces_ref.dtype)


def split_blocks(queries, digits, blocks, size, owners):
    cols = queries.shape[1]
    rows = size // owners * blocks

    def kernel(q_ref, digits_ref, pieces_ref, wide):
        wide[...] = q_ref[...].astype(jnp.float32)
        rows_to_pieces(wide, pieces_ref, blocks, size, owners)
        for k in range(owners):
            pieces_ref[k, rows:, :] = jnp.broadcast_to(digits_ref[...], (8, cols)).astype(pieces_ref.dtype)

    return pl.pallas_call(
        kernel,
        out_shape=jax.ShapeDtypeStruct((owners, rows + 8, cols), queries.dtype),
        in_specs=[VMEM, VMEM],
        out_specs=VMEM,
        scratch_shapes=[pltpu.VMEM(queries.shape, jnp.float32)],
        name="split_blocks",
    )(queries, digits)


def select_pieces(held, slots, after, wanted=None):
    devices, height, cols = held.shape
    blocks = height // 16 * 8
    parts = 2
    block_total = devices * blocks
    group = 8

    def kernel(held_ref, *rest):
        rest = rest[len(after) :]
        if wanted is None:
            out_ref, wanted_out, flat = rest
            digits = held_ref[:, parts * blocks :, :].astype(jnp.float32)[:, 0, :].T
            ids = (digits[:slots] * BASE + digits[slots : 2 * slots]).astype(jnp.int32)
            wanted_out[...] = ids
        else:
            wanted_ref, out_ref, flat = rest
            ids = wanted_ref[...]
        for s in range(devices):
            for part in range(parts):
                flat[s * blocks : (s + 1) * blocks, part * cols : (part + 1) * cols] = held_ref[
                    s, part * blocks : (part + 1) * blocks, :
                ]
        column = lax.broadcasted_iota(jnp.int32, (slots, block_total), 1)
        for first in range(0, devices, group):
            hits = [
                jnp.where(
                    jnp.broadcast_to(ids[:, d : d + 1], (slots, block_total)) == column, 1.0, 0.0
                ).astype(held.dtype)
                for d in range(first, first + group)
            ]
            out_ref[first * slots : (first + group) * slots, :] = jnp.dot(
                jnp.concatenate(hits, axis=0), flat[...], preferred_element_type=jnp.float32
            ).astype(out_ref.dtype)

    out_shape = [jax.ShapeDtypeStruct((devices * slots, parts * cols), held.dtype)]
    if wanted is None:
        out_shape.append(jax.ShapeDtypeStruct((slots, devices), jnp.int32))
    operands = () if wanted is None else (wanted,)
    return pl.pallas_call(
        kernel,
        out_shape=out_shape,
        in_specs=[VMEM] + [HBM] * len(after) + [VMEM] * len(operands),
        out_specs=[VMEM] * len(out_shape),
        scratch_shapes=[pltpu.VMEM((block_total, parts * cols), held.dtype)],
        compiler_params=pltpu.CompilerParams(vmem_limit_bytes=LIMIT),
        cost_estimate=pl.CostEstimate(
            flops=2 * devices * slots * block_total * parts * cols, bytes_accessed=2 << 20, transcendentals=0
        ),
        name="select_pieces",
    )(held, *in_hbm(after), *operands)


def near_product(near_index, counts, quarters, low, own, high):
    blocks, _, rows, size = quarters[0][0].shape
    slots = near_index.shape[1]
    cols = own.shape[2]
    group = 4
    number = len(quarters)
    near = [t for t in range(slots) if t not in FAR]
    flat = [part for quarter in quarters for part in quarter]

    def kernel(index_ref, count_ref, *refs):
        parts = iter(refs)
        tiles = [[next(parts) for _ in quarter] for quarter in quarters]
        low_ref, own_ref, high_ref, out_ref, panels, sems = parts
        step = pl.program_id(0)

        @pl.when(step == 0)
        def _():
            copies = [
                pltpu.make_async_copy(low_ref, panels.at[:EDGE], sems.at[0]),
                pltpu.make_async_copy(own_ref, panels.at[EDGE : EDGE + blocks], sems.at[1]),
                pltpu.make_async_copy(high_ref, panels.at[EDGE + blocks :], sems.at[2]),
            ]
            for copy in copies:
                copy.start()
            for copy in copies:
                copy.wait()

        for r in range(group):
            b = step * group + r
            total = jnp.zeros((number * rows, cols), jnp.float32)
            for first in range(0, len(near), 2):
                left, right = [], []
                for t in near[first : first + 2]:
                    tile = jnp.concatenate(
                        [quarter[t * len(quarter) // slots][r, t % (slots // len(quarter))] for quarter in tiles],
                        axis=0,
                    )
                    left.append(jnp.where(t < count_ref[b], tile, jnp.zeros_like(tile)))
                    right.append(panels[index_ref[b, t]])
                total += jnp.dot(
                    jnp.concatenate(left, axis=1),
                    jnp.concatenate(right, axis=0),
                    preferred_element_type=jnp.float32,
                )
            out_ref[r] = total

    return pl.pallas_call(
        kernel,
        out_shape=jax.ShapeDtypeStruct((blocks, number * rows, cols), jnp.float32),
        grid_spec=pltpu.PrefetchScalarGridSpec(
            num_scalar_prefetch=2,
            grid=(blocks // group,),
            in_specs=[
                pl.BlockSpec((group,) + part.shape[1:], lambda i, *_: (i, 0, 0, 0)) for part in flat
            ]
            + [HBM] * 3,
            out_specs=pl.BlockSpec((group, number * rows, cols), lambda i, *_: (i, 0, 0)),
            scratch_shapes=[
                pltpu.VMEM((blocks + 2 * EDGE, size, cols), own.dtype),
                pltpu.SemaphoreType.DMA((3,)),
            ],
        ),
        compiler_params=pltpu.CompilerParams(vmem_limit_bytes=LIMIT),
        cost_estimate=pl.CostEstimate(
            flops=2 * blocks * len(near) * number * rows * size * cols,
            bytes_accessed=number << 21,
            transcendentals=0,
        ),
        name="near_product",
    )(near_index, counts, *flat, *in_hbm([low, own, high]))


def add_far(offsets, counts, far_tiles, arrived, partials, queries, owners, split):
    blocks, _, rows, size = far_tiles[0].shape
    cols = queries.shape[1]
    far = arrived.shape[0] // owners
    number = len(far_tiles)

    def kernel(offset_ref, count_ref, *refs):
        tile_refs, partial_refs = refs[:number], refs[number : number + len(partials)]
        arrived_ref, q_ref, out_ref = refs[number + len(partials) : number + len(partials) + 3]
        rest = refs[number + len(partials) + 3 :]
        if split:
            pieces_ref, upper, lower, tiles, sums, sems, wide = rest
        else:
            upper, lower, tiles, sums, sems = rest
        copies = [
            pltpu.make_async_copy(ref.at[:, FAR[0] : FAR[-1] + 1], tiles.at[n], sems.at[0, n])
            for n, ref in enumerate(tile_refs)
        ]
        first = 0
        for n, (ref, part) in enumerate(zip(partial_refs, partials)):
            copies.append(
                pltpu.make_async_copy(ref, sums.at[:, first : first + part.shape[1]], sems.at[1, n])
            )
            first += part.shape[1]
        for copy in copies:
            copy.start()
        upper[...] = arrived_ref[:, :cols].astype(jnp.float32)
        lower[...] = arrived_ref[:, cols:].astype(jnp.float32)
        for copy in copies:
            copy.wait()
        for b in range(blocks):
            left, right = [], []
            for s, t in enumerate(FAR):
                tile = tiles[:, b, s].reshape(size, size)
                left.append(jnp.where(t < count_ref[b], tile, jnp.zeros_like(tile)))
                for half in (upper, lower):
                    right.append(half[pl.ds(2 * b + s, owners, stride=far), :].astype(queries.dtype))
            total = sums[b] + jnp.dot(
                jnp.concatenate(left, axis=1),
                jnp.concatenate(right, axis=0),
                preferred_element_type=jnp.float32,
            )
            for n in range(number):
                place = pl.ds(pl.multiple_of(b * size + offset_ref[n], rows), rows)
                result = 0.99 * total[n * rows : (n + 1) * rows] + q_ref[place, :].astype(jnp.float32)
                result = result.astype(out_ref.dtype)
                out_ref[place, :] = result
                if split:
                    wide[place, :] = result.astype(jnp.float32)
        if split:
            rows_to_pieces(wide, pieces_ref, blocks, size, owners)

    out_shape = [jax.ShapeDtypeStruct(queries.shape, queries.dtype)]
    out_specs = [pl.BlockSpec(queries.shape, lambda i, *_: (0, 0))]
    scratch = [
        pltpu.VMEM((owners * far, cols), jnp.float32),
        pltpu.VMEM((owners * far, cols), jnp.float32),
        pltpu.VMEM((number, blocks, len(FAR), rows, size), far_tiles[0].dtype),
        pltpu.VMEM((blocks, size, cols), jnp.float32),
        pltpu.SemaphoreType.DMA((2, number)),
    ]
    if split:
        shape = (owners, size // owners * blocks, cols)
        out_shape.append(jax.ShapeDtypeStruct(shape, queries.dtype))
        out_specs.append(pl.BlockSpec(shape, lambda i, *_: (0, 0, 0)))
        scratch.append(pltpu.VMEM(queries.shape, jnp.float32))
    return pl.pallas_call(
        kernel,
        out_shape=out_shape,
        grid_spec=pltpu.PrefetchScalarGridSpec(
            num_scalar_prefetch=2,
            grid=(1,),
            in_specs=[HBM] * (number + len(partials)) + [VMEM] * 2,
            out_specs=out_specs,
            scratch_shapes=scratch,
        ),
        compiler_params=pltpu.CompilerParams(vmem_limit_bytes=LIMIT),
        cost_estimate=pl.CostEstimate(
            flops=4 * blocks * size * size * cols, bytes_accessed=4 << 20, transcendentals=0
        ),
        name="add_far",
    )(offsets, counts, *in_hbm(far_tiles), *in_hbm(partials), arrived, *in_hbm([queries]))


def gather_rows(tiles):
    count = lax.axis_size("pb")
    up = [(i, (i + 1) % count) for i in range(count)]
    down = [((i + 1) % count, i) for i in range(count)]
    half = tiles.shape[1] // 2
    before = lax.ppermute(tiles, "pb", up)
    after = lax.ppermute(tiles, "pb", down)
    across = (lax.ppermute(before[:, :half], "pb", up), lax.ppermute(after[:, half:], "pb", down))
    return [(tiles,), (before,), (after,), across]


def on_device(affinity_tiles, block_ids, valid_counts, queries):
    blocks, slots = block_ids.shape
    rows, size = affinity_tiles.shape[2:]
    cols = queries.shape[1]
    owners = lax.axis_size("db")
    first_block = lax.axis_index("db") * blocks
    quarters = gather_rows(affinity_tiles)
    far_tiles = [pair[0] for pair in quarters]
    place = lax.axis_index("pb")
    offsets = jnp.stack([(place + shift) % lax.axis_size("pb") * rows for shift in (0, -1, 1, 2)])
    near_index = jnp.clip(block_ids - first_block + EDGE, 0, blocks + 2 * EDGE - 1)
    far = block_ids[:, FAR[0] : FAR[-1] + 1].reshape(1, -1)
    slots = far.shape[1]
    digits = jnp.concatenate([far // BASE, far % BASE], axis=1).astype(jnp.float32)
    digits = jnp.pad(digits, ((0, 0), (0, cols - 2 * slots)))
    up = [(i, i + 1) for i in range(owners - 1)]
    down = [(i + 1, i) for i in range(owners - 1)]
    ranking, wanted = queries, None
    pieces = split_blocks(queries, digits, blocks, size, owners)
    for step in range(ITERS):
        own = ranking.reshape(blocks, size, cols)
        held = lax.all_to_all(pieces, "db", split_axis=0, concat_axis=0, tiled=True)
        low = lax.ppermute(own[blocks - EDGE :], "db", up)
        high = lax.ppermute(own[:EDGE], "db", down)
        if wanted is None:
            chosen, wanted = select_pieces(held, slots, [low, high])
        else:
            (chosen,) = select_pieces(held, slots, [low, high], wanted)
        arrived = lax.all_to_all(
            chosen.reshape(owners, slots, -1), "db", split_axis=0, concat_axis=0, tiled=True
        ).reshape(chosen.shape)
        partials = [
            near_product(near_index, valid_counts, part, low, own, high)
            for part in ([quarters[:3], quarters[3:]] if step == 0 else [quarters])
        ]
        done = add_far(offsets, valid_counts, far_tiles, arrived, partials, queries, owners, step < ITERS - 1)
        ranking = done[0]
        pieces = done[-1]
    return ranking


def solution(mesh):
    return jax.shard_map(
        on_device,
        mesh=mesh,
        in_specs=(P("db", None, "pb", None), P("db", None), P("db"), P("db", "pb")),
        out_specs=P("db", "pb"),
        check_vma=False,
    )
```

```python
import jax
import jax.numpy as jnp
from jax import lax
from jax.experimental import pallas as pl
from jax.experimental.pallas import tpu as pltpu
from jax.sharding import PartitionSpec as P

EDGE = 2
ITERS = 2
BASE = 256
FAR = (1, 2)
VMEM = pl.BlockSpec(memory_space=pltpu.VMEM)
HBM = pl.BlockSpec(memory_space=pltpu.HBM)
LIMIT = 12 << 20


def in_hbm(arrays):
    return [pltpu.with_memory_space_constraint(array, pltpu.HBM) for array in arrays]


def rows_to_pieces(wide, pieces_ref, blocks, size, owners):
    for k in range(owners):
        for part in range(size // owners):
            rows = wide[pl.ds(part * owners + k, blocks, stride=size), :]
            pieces_ref[k, part * blocks : (part + 1) * blocks, :] = rows.astype(pieces_ref.dtype)


def split_blocks(queries, digits, blocks, size, owners):
    cols = queries.shape[1]
    rows = size // owners * blocks

    def kernel(q_ref, digits_ref, pieces_ref, wide):
        wide[...] = q_ref[...].astype(jnp.float32)
        rows_to_pieces(wide, pieces_ref, blocks, size, owners)
        for k in range(owners):
            pieces_ref[k, rows:, :] = jnp.broadcast_to(digits_ref[...], (8, cols)).astype(pieces_ref.dtype)

    return pl.pallas_call(
        kernel,
        out_shape=jax.ShapeDtypeStruct((owners, rows + 8, cols), queries.dtype),
        in_specs=[VMEM, VMEM],
        out_specs=VMEM,
        scratch_shapes=[pltpu.VMEM(queries.shape, jnp.float32)],
        name="split_blocks",
    )(queries, digits)


def select_pieces(held, slots, after, wanted=None):
    devices, height, cols = held.shape
    blocks = height // 16 * 8
    parts = 2
    block_total = devices * blocks
    group = 8

    def kernel(held_ref, *rest):
        rest = rest[len(after) :]
        if wanted is None:
            out_ref, wanted_out, flat = rest
            digits = held_ref[:, parts * blocks :, :].astype(jnp.float32)[:, 0, :].T
            ids = (digits[:slots] * BASE + digits[slots : 2 * slots]).astype(jnp.int32)
            wanted_out[...] = ids
        else:
            wanted_ref, out_ref, flat = rest
            ids = wanted_ref[...]
        for s in range(devices):
            for part in range(parts):
                flat[s * blocks : (s + 1) * blocks, part * cols : (part + 1) * cols] = held_ref[
                    s, part * blocks : (part + 1) * blocks, :
                ]
        column = lax.broadcasted_iota(jnp.int32, (slots, block_total), 1)
        for first in range(0, devices, group):
            hits = [
                jnp.where(
                    jnp.broadcast_to(ids[:, d : d + 1], (slots, block_total)) == column, 1.0, 0.0
                ).astype(held.dtype)
                for d in range(first, first + group)
            ]
            out_ref[first * slots : (first + group) * slots, :] = jnp.dot(
                jnp.concatenate(hits, axis=0), flat[...], preferred_element_type=jnp.float32
            ).astype(out_ref.dtype)

    out_shape = [jax.ShapeDtypeStruct((devices * slots, parts * cols), held.dtype)]
    if wanted is None:
        out_shape.append(jax.ShapeDtypeStruct((slots, devices), jnp.int32))
    operands = () if wanted is None else (wanted,)
    return pl.pallas_call(
        kernel,
        out_shape=out_shape,
        in_specs=[VMEM] + [HBM] * len(after) + [VMEM] * len(operands),
        out_specs=[VMEM] * len(out_shape),
        scratch_shapes=[pltpu.VMEM((block_total, parts * cols), held.dtype)],
        compiler_params=pltpu.CompilerParams(vmem_limit_bytes=LIMIT),
        cost_estimate=pl.CostEstimate(
            flops=2 * devices * slots * block_total * parts * cols, bytes_accessed=2 << 20, transcendentals=0
        ),
        name="select_pieces",
    )(held, *in_hbm(after), *operands)


def near_product(near_index, counts, quarters, reach):
    blocks, _, rows, size = quarters[0][0].shape
    slots = near_index.shape[1]
    cols = reach[0].shape[2]
    dtype = reach[0].dtype
    group = 4
    number = len(quarters)
    near = [t for t in range(slots) if t not in FAR]
    flat = [part for quarter in quarters for part in quarter]

    def kernel(index_ref, count_ref, *refs):
        parts = iter(refs)
        tiles = [[next(parts) for _ in quarter] for quarter in quarters]
        *reach_refs, out_ref, panels, sems = parts
        step = pl.program_id(0)

        @pl.when(step == 0)
        def _():
            copies, first = [], 0
            for n, (ref, array) in enumerate(zip(reach_refs, reach)):
                target = panels.at[first : first + array.shape[0]]
                copies.append(pltpu.make_async_copy(ref, target, sems.at[n]))
                first += array.shape[0]
            for copy in copies:
                copy.start()
            for copy in copies:
                copy.wait()

        for r in range(group):
            b = step * group + r
            total = jnp.zeros((number * rows, cols), jnp.float32)
            for first in range(0, len(near), 2):
                left, right = [], []
                for t in near[first : first + 2]:
                    tile = jnp.concatenate(
                        [quarter[t * len(quarter) // slots][r, t % (slots // len(quarter))] for quarter in tiles],
                        axis=0,
                    )
                    left.append(jnp.where(t < count_ref[b], tile, jnp.zeros_like(tile)))
                    right.append(panels[index_ref[b, t]])
                total += jnp.dot(
                    jnp.concatenate(left, axis=1),
                    jnp.concatenate(right, axis=0),
                    preferred_element_type=jnp.float32,
                )
            out_ref[r] = total

    return pl.pallas_call(
        kernel,
        out_shape=jax.ShapeDtypeStruct((blocks, number * rows, cols), jnp.float32),
        grid_spec=pltpu.PrefetchScalarGridSpec(
            num_scalar_prefetch=2,
            grid=(blocks // group,),
            in_specs=[
                pl.BlockSpec((group,) + part.shape[1:], lambda i, *_: (i, 0, 0, 0)) for part in flat
            ]
            + [HBM] * len(reach),
            out_specs=pl.BlockSpec((group, number * rows, cols), lambda i, *_: (i, 0, 0)),
            scratch_shapes=[
                pltpu.VMEM((blocks + 2 * EDGE, size, cols), dtype),
                pltpu.SemaphoreType.DMA((len(reach),)),
            ],
        ),
        compiler_params=pltpu.CompilerParams(vmem_limit_bytes=LIMIT),
        cost_estimate=pl.CostEstimate(
            flops=2 * blocks * len(near) * number * rows * size * cols,
            bytes_accessed=number << 21,
            transcendentals=0,
        ),
        name="near_product",
    )(near_index, counts, *flat, *in_hbm(reach))


def add_far(offsets, counts, far_tiles, arrived, partials, queries, owners, split):
    blocks, _, rows, size = far_tiles[0].shape
    cols = queries.shape[1]
    far = arrived.shape[0] // owners
    number = len(far_tiles)

    def kernel(offset_ref, count_ref, *refs):
        tile_refs, partial_refs = refs[:number], refs[number : number + len(partials)]
        arrived_ref, q_ref, out_ref = refs[number + len(partials) : number + len(partials) + 3]
        rest = refs[number + len(partials) + 3 :]
        if split:
            pieces_ref, upper, lower, tiles, sums, sems, wide = rest
        else:
            upper, lower, tiles, sums, sems = rest
        copies = [
            pltpu.make_async_copy(
                ref if part.shape[1] == len(FAR) else ref.at[:, FAR[0] : FAR[-1] + 1], tiles.at[n], sems.at[0, n]
            )
            for n, (ref, part) in enumerate(zip(tile_refs, far_tiles))
        ]
        first = 0
        for n, (ref, part) in enumerate(zip(partial_refs, partials)):
            copies.append(
                pltpu.make_async_copy(ref, sums.at[:, first : first + part.shape[1]], sems.at[1, n])
            )
            first += part.shape[1]
        for copy in copies:
            copy.start()
        upper[...] = arrived_ref[:, :cols].astype(jnp.float32)
        lower[...] = arrived_ref[:, cols:].astype(jnp.float32)
        for copy in copies:
            copy.wait()
        for b in range(blocks):
            left, right = [], []
            for s, t in enumerate(FAR):
                tile = tiles[:, b, s].reshape(size, size)
                left.append(jnp.where(t < count_ref[b], tile, jnp.zeros_like(tile)))
                for half in (upper, lower):
                    right.append(half[pl.ds(2 * b + s, owners, stride=far), :].astype(queries.dtype))
            total = sums[b] + jnp.dot(
                jnp.concatenate(left, axis=1),
                jnp.concatenate(right, axis=0),
                preferred_element_type=jnp.float32,
            )
            for n in range(number):
                place = pl.ds(pl.multiple_of(b * size + offset_ref[n], rows), rows)
                result = 0.99 * total[n * rows : (n + 1) * rows] + q_ref[place, :].astype(jnp.float32)
                result = result.astype(out_ref.dtype)
                out_ref[place, :] = result
                if split:
                    wide[place, :] = result.astype(jnp.float32)
        if split:
            rows_to_pieces(wide, pieces_ref, blocks, size, owners)

    out_shape = [jax.ShapeDtypeStruct(queries.shape, queries.dtype)]
    out_specs = [pl.BlockSpec(queries.shape, lambda i, *_: (0, 0))]
    scratch = [
        pltpu.VMEM((owners * far, cols), jnp.float32),
        pltpu.VMEM((owners * far, cols), jnp.float32),
        pltpu.VMEM((number, blocks, len(FAR), rows, size), far_tiles[0].dtype),
        pltpu.VMEM((blocks, size, cols), jnp.float32),
        pltpu.SemaphoreType.DMA((2, number)),
    ]
    if split:
        shape = (owners, size // owners * blocks, cols)
        out_shape.append(jax.ShapeDtypeStruct(shape, queries.dtype))
        out_specs.append(pl.BlockSpec(shape, lambda i, *_: (0, 0, 0)))
        scratch.append(pltpu.VMEM(queries.shape, jnp.float32))
    return pl.pallas_call(
        kernel,
        out_shape=out_shape,
        grid_spec=pltpu.PrefetchScalarGridSpec(
            num_scalar_prefetch=2,
            grid=(1,),
            in_specs=[HBM] * (number + len(partials)) + [VMEM] * 2,
            out_specs=out_specs,
            scratch_shapes=scratch,
        ),
        compiler_params=pltpu.CompilerParams(vmem_limit_bytes=LIMIT),
        cost_estimate=pl.CostEstimate(
            flops=4 * blocks * size * size * cols, bytes_accessed=4 << 20, transcendentals=0
        ),
        name="add_far",
    )(offsets, counts, *in_hbm(far_tiles), *in_hbm(partials), arrived, *in_hbm([queries]))


def on_device(affinity_tiles, block_ids, valid_counts, queries):
    blocks, slots = block_ids.shape
    rows, size = affinity_tiles.shape[2:]
    cols = queries.shape[1]
    owners = lax.axis_size("db")
    first_block = lax.axis_index("db") * blocks
    count = lax.axis_size("pb")
    forth = [(i, (i + 1) % count) for i in range(count)]
    back = [((i + 1) % count, i) for i in range(count)]
    opposite = [(i, (i + 2) % count) for i in range(count)]
    before = lax.ppermute(affinity_tiles, "pb", forth)
    after = lax.ppermute(affinity_tiles, "pb", back)
    across_far = lax.ppermute(affinity_tiles[:, FAR[0] : FAR[-1] + 1], "pb", opposite)
    far_tiles = [affinity_tiles, before, after, across_far]
    place = lax.axis_index("pb")
    offsets = jnp.stack([(place + shift) % count * rows for shift in (0, -1, 1, 2)])
    near_index = jnp.clip(block_ids - first_block + EDGE, 0, blocks + 2 * EDGE - 1)
    far = block_ids[:, FAR[0] : FAR[-1] + 1].reshape(1, -1)
    slots = far.shape[1]
    digits = jnp.concatenate([far // BASE, far % BASE], axis=1).astype(jnp.float32)
    digits = jnp.pad(digits, ((0, 0), (0, cols - 2 * slots)))
    up = [(i, i + 1) for i in range(owners - 1)]
    down = [(i + 1, i) for i in range(owners - 1)]
    ranking, wanted = queries, None
    pieces = split_blocks(queries, digits, blocks, size, owners)
    for step in range(ITERS):
        own = ranking.reshape(blocks, size, cols)
        held = lax.all_to_all(pieces, "db", split_axis=0, concat_axis=0, tiled=True)
        low = lax.ppermute(own[blocks - EDGE :], "db", up)
        high = lax.ppermute(own[:EDGE], "db", down)
        beyond = lax.ppermute(own, "pb", opposite)
        if wanted is None:
            chosen, wanted = select_pieces(held, slots, [low, high])
        else:
            (chosen,) = select_pieces(held, slots, [low, high, beyond], wanted)
        arrived = lax.all_to_all(
            chosen.reshape(owners, slots, -1), "db", split_axis=0, concat_axis=0, tiled=True
        ).reshape(chosen.shape)
        reach = [lax.ppermute(low, "pb", opposite), beyond, lax.ppermute(high, "pb", opposite)]
        product = near_product(near_index, valid_counts, [(affinity_tiles,)], reach)
        product, sides = lax.optimization_barrier((product, (before, after)))
        quarters = [(affinity_tiles,), (sides[0],), (sides[1],)]
        partials = [
            near_product(near_index, valid_counts, quarters, [low, own, high]),
            lax.ppermute(product, "pb", opposite),
        ]
        done = add_far(offsets, valid_counts, far_tiles, arrived, partials, queries, owners, step < ITERS - 1)
        ranking = done[0]
        pieces = done[-1]
    return ranking


def solution(mesh):
    return jax.shard_map(
        on_device,
        mesh=mesh,
        in_specs=(P("db", None, "pb", None), P("db", None), P("db"), P("db", "pb")),
        out_specs=P("db", "pb"),
        check_vma=False,
    )
```

```python
import jax
import jax.numpy as jnp
from jax import lax
from jax.experimental import pallas as pl
from jax.experimental.pallas import tpu as pltpu
from jax.sharding import PartitionSpec as P

EDGE = 2
ITERS = 2
BASE = 256
FAR = (1, 2)
VMEM = pl.BlockSpec(memory_space=pltpu.VMEM)
HBM = pl.BlockSpec(memory_space=pltpu.HBM)
LIMIT = 12 << 20


def in_hbm(arrays):
    return [pltpu.with_memory_space_constraint(array, pltpu.HBM) for array in arrays]


def rows_to_pieces(wide, pieces_ref, blocks, size, owners):
    for k in range(owners):
        for part in range(size // owners):
            rows = wide[pl.ds(part * owners + k, blocks, stride=size), :]
            pieces_ref[k, part * blocks : (part + 1) * blocks, :] = rows.astype(pieces_ref.dtype)


def split_blocks(queries, digits, blocks, size, owners):
    cols = queries.shape[1]
    rows = size // owners * blocks

    def kernel(q_ref, digits_ref, pieces_ref, wide):
        wide[...] = q_ref[...].astype(jnp.float32)
        rows_to_pieces(wide, pieces_ref, blocks, size, owners)
        for k in range(owners):
            pieces_ref[k, rows:, :] = jnp.broadcast_to(digits_ref[...], (8, cols)).astype(pieces_ref.dtype)

    return pl.pallas_call(
        kernel,
        out_shape=jax.ShapeDtypeStruct((owners, rows + 8, cols), queries.dtype),
        in_specs=[VMEM, VMEM],
        out_specs=VMEM,
        scratch_shapes=[pltpu.VMEM(queries.shape, jnp.float32)],
        name="split_blocks",
    )(queries, digits)


def select_pieces(held, slots, after, wanted=None):
    devices, height, cols = held.shape
    blocks = height // 16 * 8
    parts = 2
    block_total = devices * blocks
    group = 8

    def kernel(held_ref, *rest):
        rest = rest[len(after) :]
        if wanted is None:
            out_ref, wanted_out, flat = rest
            digits = held_ref[:, parts * blocks :, :].astype(jnp.float32)[:, 0, :].T
            ids = (digits[:slots] * BASE + digits[slots : 2 * slots]).astype(jnp.int32)
            wanted_out[...] = ids
        else:
            wanted_ref, out_ref, flat = rest
            ids = wanted_ref[...]
        for s in range(devices):
            for part in range(parts):
                flat[s * blocks : (s + 1) * blocks, part * cols : (part + 1) * cols] = held_ref[
                    s, part * blocks : (part + 1) * blocks, :
                ]
        column = lax.broadcasted_iota(jnp.int32, (slots, block_total), 1)
        for first in range(0, devices, group):
            hits = [
                jnp.where(
                    jnp.broadcast_to(ids[:, d : d + 1], (slots, block_total)) == column, 1.0, 0.0
                ).astype(held.dtype)
                for d in range(first, first + group)
            ]
            out_ref[first * slots : (first + group) * slots, :] = jnp.dot(
                jnp.concatenate(hits, axis=0), flat[...], preferred_element_type=jnp.float32
            ).astype(out_ref.dtype)

    out_shape = [jax.ShapeDtypeStruct((devices * slots, parts * cols), held.dtype)]
    if wanted is None:
        out_shape.append(jax.ShapeDtypeStruct((slots, devices), jnp.int32))
    operands = () if wanted is None else (wanted,)
    return pl.pallas_call(
        kernel,
        out_shape=out_shape,
        in_specs=[VMEM] + [HBM] * len(after) + [VMEM] * len(operands),
        out_specs=[VMEM] * len(out_shape),
        scratch_shapes=[pltpu.VMEM((block_total, parts * cols), held.dtype)],
        compiler_params=pltpu.CompilerParams(vmem_limit_bytes=LIMIT),
        cost_estimate=pl.CostEstimate(
            flops=2 * devices * slots * block_total * parts * cols, bytes_accessed=2 << 20, transcendentals=0
        ),
        name="select_pieces",
    )(held, *in_hbm(after), *operands)


def near_product(near_index, counts, quarters, reach):
    blocks, _, rows, size = quarters[0][0].shape
    slots = near_index.shape[1]
    cols = reach[0].shape[2]
    dtype = reach[0].dtype
    group = 4
    number = len(quarters)
    near = [t for t in range(slots) if t not in FAR]
    flat = [part for quarter in quarters for part in quarter]

    def kernel(index_ref, count_ref, *refs):
        parts = iter(refs)
        tiles = [[next(parts) for _ in quarter] for quarter in quarters]
        *reach_refs, out_ref, panels, sems = parts
        step = pl.program_id(0)

        @pl.when(step == 0)
        def _():
            copies, first = [], 0
            for n, (ref, array) in enumerate(zip(reach_refs, reach)):
                target = panels.at[first : first + array.shape[0]]
                copies.append(pltpu.make_async_copy(ref, target, sems.at[n]))
                first += array.shape[0]
            for copy in copies:
                copy.start()
            for copy in copies:
                copy.wait()

        for r in range(group):
            b = step * group + r
            total = jnp.zeros((number * rows, cols), jnp.float32)
            for first in range(0, len(near), 2):
                left, right = [], []
                for t in near[first : first + 2]:
                    tile = jnp.concatenate(
                        [quarter[t * len(quarter) // slots][r, t % (slots // len(quarter))] for quarter in tiles],
                        axis=0,
                    )
                    left.append(jnp.where(t < count_ref[b], tile, jnp.zeros_like(tile)))
                    right.append(panels[index_ref[b, t]])
                total += jnp.dot(
                    jnp.concatenate(left, axis=1),
                    jnp.concatenate(right, axis=0),
                    preferred_element_type=jnp.float32,
                )
            out_ref[r] = total

    return pl.pallas_call(
        kernel,
        out_shape=jax.ShapeDtypeStruct((blocks, number * rows, cols), jnp.float32),
        grid_spec=pltpu.PrefetchScalarGridSpec(
            num_scalar_prefetch=2,
            grid=(blocks // group,),
            in_specs=[
                pl.BlockSpec((group,) + part.shape[1:], lambda i, *_: (i, 0, 0, 0)) for part in flat
            ]
            + [HBM] * len(reach),
            out_specs=pl.BlockSpec((group, number * rows, cols), lambda i, *_: (i, 0, 0)),
            scratch_shapes=[
                pltpu.VMEM((blocks + 2 * EDGE, size, cols), dtype),
                pltpu.SemaphoreType.DMA((len(reach),)),
            ],
        ),
        compiler_params=pltpu.CompilerParams(vmem_limit_bytes=LIMIT),
        cost_estimate=pl.CostEstimate(
            flops=2 * blocks * len(near) * number * rows * size * cols,
            bytes_accessed=number << 21,
            transcendentals=0,
        ),
        name="near_product",
    )(near_index, counts, *flat, *in_hbm(reach))


def add_far(offsets, counts, far_tiles, arrived, partials, queries, owners, split):
    blocks, _, rows, size = far_tiles[0].shape
    cols = queries.shape[1]
    far = arrived.shape[0] // owners
    number = len(far_tiles)

    def kernel(offset_ref, count_ref, *refs):
        tile_refs, partial_refs = refs[:number], refs[number : number + len(partials)]
        arrived_ref, q_ref, out_ref = refs[number + len(partials) : number + len(partials) + 3]
        rest = refs[number + len(partials) + 3 :]
        if split:
            pieces_ref, upper, lower, tiles, sums, sems, wide = rest
        else:
            upper, lower, tiles, sums, sems = rest
        copies = [
            pltpu.make_async_copy(
                ref if part.shape[1] == len(FAR) else ref.at[:, FAR[0] : FAR[-1] + 1], tiles.at[n], sems.at[0, n]
            )
            for n, (ref, part) in enumerate(zip(tile_refs, far_tiles))
        ]
        first = 0
        for n, (ref, part) in enumerate(zip(partial_refs, partials)):
            copies.append(
                pltpu.make_async_copy(ref, sums.at[:, first : first + part.shape[1]], sems.at[1, n])
            )
            first += part.shape[1]
        for copy in copies:
            copy.start()
        upper[...] = arrived_ref[:, :cols].astype(jnp.float32)
        lower[...] = arrived_ref[:, cols:].astype(jnp.float32)
        for copy in copies:
            copy.wait()
        for b in range(blocks):
            left, right = [], []
            for s, t in enumerate(FAR):
                tile = tiles[:, b, s].reshape(size, size)
                left.append(jnp.where(t < count_ref[b], tile, jnp.zeros_like(tile)))
                for half in (upper, lower):
                    right.append(half[pl.ds(2 * b + s, owners, stride=far), :].astype(queries.dtype))
            total = sums[b] + jnp.dot(
                jnp.concatenate(left, axis=1),
                jnp.concatenate(right, axis=0),
                preferred_element_type=jnp.float32,
            )
            for n in range(number):
                place = pl.ds(pl.multiple_of(b * size + offset_ref[n], rows), rows)
                result = 0.99 * total[n * rows : (n + 1) * rows] + q_ref[place, :].astype(jnp.float32)
                result = result.astype(out_ref.dtype)
                out_ref[place, :] = result
                if split:
                    wide[place, :] = result.astype(jnp.float32)
        if split:
            rows_to_pieces(wide, pieces_ref, blocks, size, owners)

    out_shape = [jax.ShapeDtypeStruct(queries.shape, queries.dtype)]
    out_specs = [pl.BlockSpec(queries.shape, lambda i, *_: (0, 0))]
    scratch = [
        pltpu.VMEM((owners * far, cols), jnp.float32),
        pltpu.VMEM((owners * far, cols), jnp.float32),
        pltpu.VMEM((number, blocks, len(FAR), rows, size), far_tiles[0].dtype),
        pltpu.VMEM((blocks, size, cols), jnp.float32),
        pltpu.SemaphoreType.DMA((2, number)),
    ]
    if split:
        shape = (owners, size // owners * blocks, cols)
        out_shape.append(jax.ShapeDtypeStruct(shape, queries.dtype))
        out_specs.append(pl.BlockSpec(shape, lambda i, *_: (0, 0, 0)))
        scratch.append(pltpu.VMEM(queries.shape, jnp.float32))
    return pl.pallas_call(
        kernel,
        out_shape=out_shape,
        grid_spec=pltpu.PrefetchScalarGridSpec(
            num_scalar_prefetch=2,
            grid=(1,),
            in_specs=[HBM] * (number + len(partials)) + [VMEM] * 2,
            out_specs=out_specs,
            scratch_shapes=scratch,
        ),
        compiler_params=pltpu.CompilerParams(vmem_limit_bytes=LIMIT),
        cost_estimate=pl.CostEstimate(
            flops=4 * blocks * size * size * cols, bytes_accessed=4 << 20, transcendentals=0
        ),
        name="add_far",
    )(offsets, counts, *in_hbm(far_tiles), *in_hbm(partials), arrived, *in_hbm([queries]))


def on_device(affinity_tiles, block_ids, valid_counts, queries):
    blocks, slots = block_ids.shape
    rows, size = affinity_tiles.shape[2:]
    cols = queries.shape[1]
    owners = lax.axis_size("db")
    first_block = lax.axis_index("db") * blocks
    count = lax.axis_size("pb")
    forth = [(i, (i + 1) % count) for i in range(count)]
    back = [((i + 1) % count, i) for i in range(count)]
    opposite = [(i, (i + 2) % count) for i in range(count)]
    before = lax.ppermute(affinity_tiles, "pb", forth)
    after = lax.ppermute(affinity_tiles, "pb", back)
    across_far = lax.ppermute(affinity_tiles[:, FAR[0] : FAR[-1] + 1], "pb", opposite)
    far_tiles = [affinity_tiles, before, after, across_far]
    place = lax.axis_index("pb")
    offsets = jnp.stack([(place + shift) % count * rows for shift in (0, -1, 1, 2)])
    near_index = jnp.clip(block_ids - first_block + EDGE, 0, blocks + 2 * EDGE - 1)
    far = block_ids[:, FAR[0] : FAR[-1] + 1].reshape(1, -1)
    slots = far.shape[1]
    digits = jnp.concatenate([far // BASE, far % BASE], axis=1).astype(jnp.float32)
    digits = jnp.pad(digits, ((0, 0), (0, cols - 2 * slots)))
    up = [(i, i + 1) for i in range(owners - 1)]
    down = [(i + 1, i) for i in range(owners - 1)]
    ranking, wanted = queries, None
    pieces = split_blocks(queries, digits, blocks, size, owners)
    for step in range(ITERS):
        own = ranking.reshape(blocks, size, cols)
        beyond = lax.ppermute(own, "pb", opposite)
        if step == 0:
            pieces, beyond = lax.optimization_barrier((pieces, beyond))
        held = lax.all_to_all(pieces, "db", split_axis=0, concat_axis=0, tiled=True)
        low = lax.ppermute(own[blocks - EDGE :], "db", up)
        high = lax.ppermute(own[:EDGE], "db", down)
        if wanted is None:
            chosen, wanted = select_pieces(held, slots, [low, high])
        else:
            (chosen,) = select_pieces(held, slots, [low, high, beyond], wanted)
        arrived = lax.all_to_all(
            chosen.reshape(owners, slots, -1), "db", split_axis=0, concat_axis=0, tiled=True
        ).reshape(chosen.shape)
        reach = [lax.ppermute(low, "pb", opposite), beyond, lax.ppermute(high, "pb", opposite)]
        product = near_product(near_index, valid_counts, [(affinity_tiles,)], reach)
        product, sides = lax.optimization_barrier((product, (before, after)))
        quarters = [(affinity_tiles,), (sides[0],), (sides[1],)]
        partials = [
            near_product(near_index, valid_counts, quarters, [low, own, high]),
            lax.ppermute(product, "pb", opposite),
        ]
        done = add_far(offsets, valid_counts, far_tiles, arrived, partials, queries, owners, step < ITERS - 1)
        ranking = done[0]
        pieces = done[-1]
    return ranking


def solution(mesh):
    return jax.shard_map(
        on_device,
        mesh=mesh,
        in_specs=(P("db", None, "pb", None), P("db", None), P("db"), P("db", "pb")),
        out_specs=P("db", "pb"),
        check_vma=False,
    )
```

```python
import jax
import jax.numpy as jnp
from jax import lax
from jax.experimental import pallas as pl
from jax.experimental.pallas import tpu as pltpu
from jax.sharding import PartitionSpec as P

EDGE = 2
ITERS = 2
BASE = 256
FAR = (1, 2)
VMEM = pl.BlockSpec(memory_space=pltpu.VMEM)
HBM = pl.BlockSpec(memory_space=pltpu.HBM)
LIMIT = 12 << 20


def in_hbm(arrays):
    return [pltpu.with_memory_space_constraint(array, pltpu.HBM) for array in arrays]


def rows_to_pieces(wide, pieces_ref, blocks, size, owners):
    for k in range(owners):
        for part in range(size // owners):
            rows = wide[pl.ds(part * owners + k, blocks, stride=size), :]
            pieces_ref[k, part * blocks : (part + 1) * blocks, :] = rows.astype(pieces_ref.dtype)


def split_blocks(queries, digits, blocks, size, owners):
    cols = queries.shape[1]
    rows = size // owners * blocks

    def kernel(q_ref, digits_ref, pieces_ref, wide):
        wide[...] = q_ref[...].astype(jnp.float32)
        rows_to_pieces(wide, pieces_ref, blocks, size, owners)
        for k in range(owners):
            pieces_ref[k, rows:, :] = jnp.broadcast_to(digits_ref[...], (8, cols)).astype(pieces_ref.dtype)

    return pl.pallas_call(
        kernel,
        out_shape=jax.ShapeDtypeStruct((owners, rows + 8, cols), queries.dtype),
        in_specs=[VMEM, VMEM],
        out_specs=VMEM,
        scratch_shapes=[pltpu.VMEM(queries.shape, jnp.float32)],
        name="split_blocks",
    )(queries, digits)


def select_pieces(held, slots, after, wanted=None):
    devices, height, cols = held.shape
    blocks = height // 16 * 8
    parts = 2
    block_total = devices * blocks
    group = 8

    def kernel(held_ref, *rest):
        rest = rest[len(after) :]
        if wanted is None:
            out_ref, wanted_out, flat = rest
            digits = held_ref[:, parts * blocks :, :].astype(jnp.float32)[:, 0, :].T
            ids = (digits[:slots] * BASE + digits[slots : 2 * slots]).astype(jnp.int32)
            wanted_out[...] = ids
        else:
            wanted_ref, out_ref, flat = rest
            ids = wanted_ref[...]
        for s in range(devices):
            for part in range(parts):
                flat[s * blocks : (s + 1) * blocks, part * cols : (part + 1) * cols] = held_ref[
                    s, part * blocks : (part + 1) * blocks, :
                ]
        column = lax.broadcasted_iota(jnp.int32, (slots, block_total), 1)
        for first in range(0, devices, group):
            hits = [
                jnp.where(
                    jnp.broadcast_to(ids[:, d : d + 1], (slots, block_total)) == column, 1.0, 0.0
                ).astype(held.dtype)
                for d in range(first, first + group)
            ]
            out_ref[first * slots : (first + group) * slots, :] = jnp.dot(
                jnp.concatenate(hits, axis=0), flat[...], preferred_element_type=jnp.float32
            ).astype(out_ref.dtype)

    out_shape = [jax.ShapeDtypeStruct((devices * slots, parts * cols), held.dtype)]
    if wanted is None:
        out_shape.append(jax.ShapeDtypeStruct((slots, devices), jnp.int32))
    operands = () if wanted is None else (wanted,)
    return pl.pallas_call(
        kernel,
        out_shape=out_shape,
        in_specs=[VMEM] + [HBM] * len(after) + [VMEM] * len(operands),
        out_specs=[VMEM] * len(out_shape),
        scratch_shapes=[pltpu.VMEM((block_total, parts * cols), held.dtype)],
        compiler_params=pltpu.CompilerParams(vmem_limit_bytes=LIMIT),
        cost_estimate=pl.CostEstimate(
            flops=2 * devices * slots * block_total * parts * cols, bytes_accessed=2 << 20, transcendentals=0
        ),
        name="select_pieces",
    )(held, *in_hbm(after), *operands)


def near_product(near_index, counts, quarters, reach):
    blocks, _, rows, size = quarters[0][0].shape
    slots = near_index.shape[1]
    cols = reach[0].shape[2]
    dtype = reach[0].dtype
    group = 4
    number = len(quarters)
    near = [t for t in range(slots) if t not in FAR]
    flat = [part for quarter in quarters for part in quarter]

    def kernel(index_ref, count_ref, *refs):
        parts = iter(refs)
        tiles = [[next(parts) for _ in quarter] for quarter in quarters]
        *reach_refs, out_ref, panels, sems = parts
        step = pl.program_id(0)

        @pl.when(step == 0)
        def _():
            copies, first = [], 0
            for n, (ref, array) in enumerate(zip(reach_refs, reach)):
                target = panels.at[first : first + array.shape[0]]
                copies.append(pltpu.make_async_copy(ref, target, sems.at[n]))
                first += array.shape[0]
            for copy in copies:
                copy.start()
            for copy in copies:
                copy.wait()

        for r in range(group):
            b = step * group + r
            total = jnp.zeros((number * rows, cols), jnp.float32)
            for first in range(0, len(near), 2):
                left, right = [], []
                for t in near[first : first + 2]:
                    tile = jnp.concatenate(
                        [quarter[t * len(quarter) // slots][r, t % (slots // len(quarter))] for quarter in tiles],
                        axis=0,
                    )
                    left.append(jnp.where(t < count_ref[b], tile, jnp.zeros_like(tile)))
                    right.append(panels[index_ref[b, t]])
                total += jnp.dot(
                    jnp.concatenate(left, axis=1),
                    jnp.concatenate(right, axis=0),
                    preferred_element_type=jnp.float32,
                )
            out_ref[r] = total

    return pl.pallas_call(
        kernel,
        out_shape=jax.ShapeDtypeStruct((blocks, number * rows, cols), jnp.float32),
        grid_spec=pltpu.PrefetchScalarGridSpec(
            num_scalar_prefetch=2,
            grid=(blocks // group,),
            in_specs=[
                pl.BlockSpec((group,) + part.shape[1:], lambda i, *_: (i, 0, 0, 0)) for part in flat
            ]
            + [HBM] * len(reach),
            out_specs=pl.BlockSpec((group, number * rows, cols), lambda i, *_: (i, 0, 0)),
            scratch_shapes=[
                pltpu.VMEM((blocks + 2 * EDGE, size, cols), dtype),
                pltpu.SemaphoreType.DMA((len(reach),)),
            ],
        ),
        compiler_params=pltpu.CompilerParams(vmem_limit_bytes=LIMIT),
        cost_estimate=pl.CostEstimate(
            flops=2 * blocks * len(near) * number * rows * size * cols,
            bytes_accessed=number << 21,
            transcendentals=0,
        ),
        name="near_product",
    )(near_index, counts, *flat, *in_hbm(reach))


def add_far(offsets, counts, far_tiles, arrived, partials, queries, owners, split):
    blocks, _, rows, size = far_tiles[0].shape
    cols = queries.shape[1]
    far = arrived.shape[0] // owners
    number = len(far_tiles)

    def kernel(offset_ref, count_ref, *refs):
        tile_refs, partial_refs = refs[:number], refs[number : number + len(partials)]
        arrived_ref, q_ref, out_ref = refs[number + len(partials) : number + len(partials) + 3]
        rest = refs[number + len(partials) + 3 :]
        if split:
            pieces_ref, upper, lower, landed, q_rows, tiles, sums, sems, wide = rest
        else:
            upper, lower, landed, q_rows, tiles, sums, sems = rest
        chunks = [slice(c * owners * far // number, (c + 1) * owners * far // number) for c in range(number)]
        landings = [
            pltpu.make_async_copy(arrived_ref.at[rows_of], landed.at[rows_of], sems.at[2, c])
            for c, rows_of in enumerate(chunks)
        ]
        for copy in landings:
            copy.start()
        copies = [
            pltpu.make_async_copy(
                ref if part.shape[1] == len(FAR) else ref.at[:, FAR[0] : FAR[-1] + 1], tiles.at[n], sems.at[0, n]
            )
            for n, (ref, part) in enumerate(zip(tile_refs, far_tiles))
        ]
        first = 0
        for n, (ref, part) in enumerate(zip(partial_refs, partials)):
            copies.append(
                pltpu.make_async_copy(ref, sums.at[:, first : first + part.shape[1]], sems.at[1, n])
            )
            first += part.shape[1]
        copies.append(pltpu.make_async_copy(q_ref, q_rows, sems.at[3, 0]))
        for copy in copies:
            copy.start()
        for copy, rows_of in zip(landings, chunks):
            copy.wait()
            upper[rows_of, :] = landed[rows_of, :cols].astype(jnp.float32)
            lower[rows_of, :] = landed[rows_of, cols:].astype(jnp.float32)
        for copy in copies:
            copy.wait()
        for b in range(blocks):
            left, right = [], []
            for s, t in enumerate(FAR):
                tile = tiles[:, b, s].reshape(size, size)
                left.append(jnp.where(t < count_ref[b], tile, jnp.zeros_like(tile)))
                for half in (upper, lower):
                    right.append(half[pl.ds(2 * b + s, owners, stride=far), :].astype(queries.dtype))
            total = sums[b] + jnp.dot(
                jnp.concatenate(left, axis=1),
                jnp.concatenate(right, axis=0),
                preferred_element_type=jnp.float32,
            )
            for n in range(number):
                place = pl.ds(pl.multiple_of(b * size + offset_ref[n], rows), rows)
                result = 0.99 * total[n * rows : (n + 1) * rows] + q_rows[place, :].astype(jnp.float32)
                result = result.astype(out_ref.dtype)
                out_ref[place, :] = result
                if split:
                    wide[place, :] = result.astype(jnp.float32)
        if split:
            rows_to_pieces(wide, pieces_ref, blocks, size, owners)

    out_shape = [jax.ShapeDtypeStruct(queries.shape, queries.dtype)]
    out_specs = [pl.BlockSpec(queries.shape, lambda i, *_: (0, 0))]
    scratch = [
        pltpu.VMEM((owners * far, cols), jnp.float32),
        pltpu.VMEM((owners * far, cols), jnp.float32),
        pltpu.VMEM(arrived.shape, arrived.dtype),
        pltpu.VMEM(queries.shape, queries.dtype),
        pltpu.VMEM((number, blocks, len(FAR), rows, size), far_tiles[0].dtype),
        pltpu.VMEM((blocks, size, cols), jnp.float32),
        pltpu.SemaphoreType.DMA((4, number)),
    ]
    if split:
        shape = (owners, size // owners * blocks, cols)
        out_shape.append(jax.ShapeDtypeStruct(shape, queries.dtype))
        out_specs.append(pl.BlockSpec(shape, lambda i, *_: (0, 0, 0)))
        scratch.append(pltpu.VMEM(queries.shape, jnp.float32))
    return pl.pallas_call(
        kernel,
        out_shape=out_shape,
        grid_spec=pltpu.PrefetchScalarGridSpec(
            num_scalar_prefetch=2,
            grid=(1,),
            in_specs=[HBM] * (number + len(partials) + 2),
            out_specs=out_specs,
            scratch_shapes=scratch,
        ),
        compiler_params=pltpu.CompilerParams(vmem_limit_bytes=LIMIT),
        cost_estimate=pl.CostEstimate(
            flops=4 * blocks * size * size * cols, bytes_accessed=4 << 20, transcendentals=0
        ),
        name="add_far",
    )(offsets, counts, *in_hbm(far_tiles), *in_hbm(partials), arrived, *in_hbm([queries]))


def on_device(affinity_tiles, block_ids, valid_counts, queries):
    blocks, slots = block_ids.shape
    rows, size = affinity_tiles.shape[2:]
    cols = queries.shape[1]
    owners = lax.axis_size("db")
    first_block = lax.axis_index("db") * blocks
    count = lax.axis_size("pb")
    forth = [(i, (i + 1) % count) for i in range(count)]
    back = [((i + 1) % count, i) for i in range(count)]
    opposite = [(i, (i + 2) % count) for i in range(count)]
    before = lax.ppermute(affinity_tiles, "pb", forth)
    after = lax.ppermute(affinity_tiles, "pb", back)
    across_far = lax.ppermute(affinity_tiles[:, FAR[0] : FAR[-1] + 1], "pb", opposite)
    far_tiles = [affinity_tiles, before, after, across_far]
    place = lax.axis_index("pb")
    offsets = jnp.stack([(place + shift) % count * rows for shift in (0, -1, 1, 2)])
    near_index = jnp.clip(block_ids - first_block + EDGE, 0, blocks + 2 * EDGE - 1)
    far = block_ids[:, FAR[0] : FAR[-1] + 1].reshape(1, -1)
    slots = far.shape[1]
    digits = jnp.concatenate([far // BASE, far % BASE], axis=1).astype(jnp.float32)
    digits = jnp.pad(digits, ((0, 0), (0, cols - 2 * slots)))
    up = [(i, i + 1) for i in range(owners - 1)]
    down = [(i + 1, i) for i in range(owners - 1)]
    ranking, wanted = queries, None
    pieces = split_blocks(queries, digits, blocks, size, owners)
    for step in range(ITERS):
        own = ranking.reshape(blocks, size, cols)
        held = lax.all_to_all(pieces, "db", split_axis=0, concat_axis=0, tiled=True)
        low = lax.ppermute(own[blocks - EDGE :], "db", up)
        high = lax.ppermute(own[:EDGE], "db", down)
        beyond = lax.ppermute(own, "pb", opposite)
        if wanted is None:
            chosen, wanted = select_pieces(held, slots, [low, high])
        else:
            (chosen,) = select_pieces(held, slots, [low, high, beyond], wanted)
        arrived = lax.all_to_all(
            chosen.reshape(owners, slots, -1), "db", split_axis=0, concat_axis=0, tiled=True
        ).reshape(chosen.shape)
        reach = [lax.ppermute(low, "pb", opposite), beyond, lax.ppermute(high, "pb", opposite)]
        product = near_product(near_index, valid_counts, [(affinity_tiles,)], reach)
        product, sides = lax.optimization_barrier((product, (before, after)))
        quarters = [(affinity_tiles,), (sides[0],), (sides[1],)]
        partials = [
            near_product(near_index, valid_counts, quarters, [low, own, high]),
            lax.ppermute(product, "pb", opposite),
        ]
        done = add_far(offsets, valid_counts, far_tiles, arrived, partials, queries, owners, step < ITERS - 1)
        ranking = done[0]
        pieces = done[-1]
    return ranking


def solution(mesh):
    return jax.shard_map(
        on_device,
        mesh=mesh,
        in_specs=(P("db", None, "pb", None), P("db", None), P("db"), P("db", "pb")),
        out_specs=P("db", "pb"),
        check_vma=False,
    )
```

```python
import jax
import jax.numpy as jnp
from jax import lax
from jax.experimental import pallas as pl
from jax.experimental.pallas import tpu as pltpu
from jax.sharding import PartitionSpec as P

EDGE = 2
ITERS = 2
BASE = 256
FAR = (1, 2)
VMEM = pl.BlockSpec(memory_space=pltpu.VMEM)
HBM = pl.BlockSpec(memory_space=pltpu.HBM)
LIMIT = 12 << 20


def in_hbm(arrays):
    return [pltpu.with_memory_space_constraint(array, pltpu.HBM) for array in arrays]


def rows_to_pieces(wide, pieces_ref, blocks, size, owners):
    for k in range(owners):
        for part in range(size // owners):
            rows = wide[pl.ds(part * owners + k, blocks, stride=size), :]
            pieces_ref[k, part * blocks : (part + 1) * blocks, :] = rows.astype(pieces_ref.dtype)


def split_blocks(queries, digits, blocks, size, owners):
    cols = queries.shape[1]
    rows = size // owners * blocks

    def kernel(q_ref, digits_ref, pieces_ref, wide):
        wide[...] = q_ref[...].astype(jnp.float32)
        rows_to_pieces(wide, pieces_ref, blocks, size, owners)
        for k in range(owners):
            pieces_ref[k, rows:, :] = jnp.broadcast_to(digits_ref[...], (8, cols)).astype(pieces_ref.dtype)

    return pl.pallas_call(
        kernel,
        out_shape=jax.ShapeDtypeStruct((owners, rows + 8, cols), queries.dtype),
        in_specs=[VMEM, VMEM],
        out_specs=VMEM,
        scratch_shapes=[pltpu.VMEM(queries.shape, jnp.float32)],
        name="split_blocks",
    )(queries, digits)


def select_pieces(held, slots, after, wanted=None):
    devices, height, cols = held.shape
    blocks = height // 16 * 8
    parts = 2
    block_total = devices * blocks
    group = 8

    def kernel(held_ref, *rest):
        rest = rest[len(after) :]
        if wanted is None:
            out_ref, wanted_out, flat, tail, sems = rest
        else:
            wanted_ref, out_ref, flat, tail, sems = rest
        copies = [
            pltpu.make_async_copy(
                held_ref.at[:, part * blocks : (part + 1) * blocks],
                flat.at[:, :, part * cols : (part + 1) * cols],
                sems.at[part],
            )
            for part in range(parts)
        ]
        for copy in copies:
            copy.start()
        if wanted is None:
            copy = pltpu.make_async_copy(held_ref.at[:, parts * blocks :], tail, sems.at[parts])
            copy.start()
            copy.wait()
            digits = tail[...].astype(jnp.float32)[:, 0, :].T
            ids = (digits[:slots] * BASE + digits[slots : 2 * slots]).astype(jnp.int32)
            wanted_out[...] = ids
        else:
            ids = wanted_ref[...]
        for copy in copies:
            copy.wait()
        column = lax.broadcasted_iota(jnp.int32, (slots, block_total), 1)
        for first in range(0, devices, group):
            hits = [
                jnp.where(
                    jnp.broadcast_to(ids[:, d : d + 1], (slots, block_total)) == column, 1.0, 0.0
                ).astype(held.dtype)
                for d in range(first, first + group)
            ]
            out_ref[first * slots : (first + group) * slots, :] = jnp.dot(
                jnp.concatenate(hits, axis=0), flat[...].reshape(block_total, -1), preferred_element_type=jnp.float32
            ).astype(out_ref.dtype)

    out_shape = [jax.ShapeDtypeStruct((devices * slots, parts * cols), held.dtype)]
    if wanted is None:
        out_shape.append(jax.ShapeDtypeStruct((slots, devices), jnp.int32))
    operands = () if wanted is None else (wanted,)
    return pl.pallas_call(
        kernel,
        out_shape=out_shape,
        in_specs=[HBM] * (1 + len(after)) + [VMEM] * len(operands),
        out_specs=[VMEM] * len(out_shape),
        scratch_shapes=[
            pltpu.VMEM((devices, blocks, parts * cols), held.dtype),
            pltpu.VMEM((devices, 8, cols), held.dtype),
            pltpu.SemaphoreType.DMA((parts + 1,)),
        ],
        compiler_params=pltpu.CompilerParams(vmem_limit_bytes=LIMIT),
        cost_estimate=pl.CostEstimate(
            flops=2 * devices * slots * block_total * parts * cols, bytes_accessed=2 << 20, transcendentals=0
        ),
        name="select_pieces",
    )(*in_hbm([held, *after]), *operands)


def near_product(near_index, counts, quarters, reach):
    blocks, _, rows, size = quarters[0][0].shape
    slots = near_index.shape[1]
    cols = reach[0].shape[2]
    dtype = reach[0].dtype
    group = 4
    number = len(quarters)
    near = [t for t in range(slots) if t not in FAR]
    flat = [part for quarter in quarters for part in quarter]

    def kernel(index_ref, count_ref, *refs):
        parts = iter(refs)
        tiles = [[next(parts) for _ in quarter] for quarter in quarters]
        *reach_refs, out_ref, panels, sems = parts
        step = pl.program_id(0)

        @pl.when(step == 0)
        def _():
            copies, first = [], 0
            for n, (ref, array) in enumerate(zip(reach_refs, reach)):
                target = panels.at[first : first + array.shape[0]]
                copies.append(pltpu.make_async_copy(ref, target, sems.at[n]))
                first += array.shape[0]
            for copy in copies:
                copy.start()
            for copy in copies:
                copy.wait()

        for r in range(group):
            b = step * group + r
            total = jnp.zeros((number * rows, cols), jnp.float32)
            for first in range(0, len(near), 2):
                left, right = [], []
                for t in near[first : first + 2]:
                    tile = jnp.concatenate(
                        [quarter[t * len(quarter) // slots][r, t % (slots // len(quarter))] for quarter in tiles],
                        axis=0,
                    )
                    left.append(jnp.where(t < count_ref[b], tile, jnp.zeros_like(tile)))
                    right.append(panels[index_ref[b, t]])
                total += jnp.dot(
                    jnp.concatenate(left, axis=1),
                    jnp.concatenate(right, axis=0),
                    preferred_element_type=jnp.float32,
                )
            out_ref[r] = total

    return pl.pallas_call(
        kernel,
        out_shape=jax.ShapeDtypeStruct((blocks, number * rows, cols), jnp.float32),
        grid_spec=pltpu.PrefetchScalarGridSpec(
            num_scalar_prefetch=2,
            grid=(blocks // group,),
            in_specs=[
                pl.BlockSpec((group,) + part.shape[1:], lambda i, *_: (i, 0, 0, 0)) for part in flat
            ]
            + [HBM] * len(reach),
            out_specs=pl.BlockSpec((group, number * rows, cols), lambda i, *_: (i, 0, 0)),
            scratch_shapes=[
                pltpu.VMEM((blocks + 2 * EDGE, size, cols), dtype),
                pltpu.SemaphoreType.DMA((len(reach),)),
            ],
        ),
        compiler_params=pltpu.CompilerParams(vmem_limit_bytes=LIMIT),
        cost_estimate=pl.CostEstimate(
            flops=2 * blocks * len(near) * number * rows * size * cols,
            bytes_accessed=number << 21,
            transcendentals=0,
        ),
        name="near_product",
    )(near_index, counts, *flat, *in_hbm(reach))


def add_far(offsets, counts, far_tiles, arrived, partials, queries, owners, split):
    blocks, _, rows, size = far_tiles[0].shape
    cols = queries.shape[1]
    far = arrived.shape[0] // owners
    number = len(far_tiles)

    def kernel(offset_ref, count_ref, *refs):
        tile_refs, partial_refs = refs[:number], refs[number : number + len(partials)]
        arrived_ref, q_ref, out_ref = refs[number + len(partials) : number + len(partials) + 3]
        rest = refs[number + len(partials) + 3 :]
        if split:
            pieces_ref, upper, lower, landed, q_rows, tiles, sums, sems, wide = rest
        else:
            upper, lower, landed, q_rows, tiles, sums, sems = rest
        chunks = [slice(c * owners * far // number, (c + 1) * owners * far // number) for c in range(number)]
        landings = [
            pltpu.make_async_copy(arrived_ref.at[rows_of], landed.at[rows_of], sems.at[2, c])
            for c, rows_of in enumerate(chunks)
        ]
        for copy in landings:
            copy.start()
        copies = [
            pltpu.make_async_copy(
                ref if part.shape[1] == len(FAR) else ref.at[:, FAR[0] : FAR[-1] + 1], tiles.at[n], sems.at[0, n]
            )
            for n, (ref, part) in enumerate(zip(tile_refs, far_tiles))
        ]
        first = 0
        for n, (ref, part) in enumerate(zip(partial_refs, partials)):
            copies.append(
                pltpu.make_async_copy(ref, sums.at[:, first : first + part.shape[1]], sems.at[1, n])
            )
            first += part.shape[1]
        copies.append(pltpu.make_async_copy(q_ref, q_rows, sems.at[3, 0]))
        for copy in copies:
            copy.start()
        for copy, rows_of in zip(landings, chunks):
            copy.wait()
            upper[rows_of, :] = landed[rows_of, :cols].astype(jnp.float32)
            lower[rows_of, :] = landed[rows_of, cols:].astype(jnp.float32)
        for copy in copies:
            copy.wait()
        for b in range(blocks):
            left, right = [], []
            for s, t in enumerate(FAR):
                tile = tiles[:, b, s].reshape(size, size)
                left.append(jnp.where(t < count_ref[b], tile, jnp.zeros_like(tile)))
                for half in (upper, lower):
                    right.append(half[pl.ds(2 * b + s, owners, stride=far), :].astype(queries.dtype))
            total = sums[b] + jnp.dot(
                jnp.concatenate(left, axis=1),
                jnp.concatenate(right, axis=0),
                preferred_element_type=jnp.float32,
            )
            for n in range(number):
                place = pl.ds(pl.multiple_of(b * size + offset_ref[n], rows), rows)
                result = 0.99 * total[n * rows : (n + 1) * rows] + q_rows[place, :].astype(jnp.float32)
                result = result.astype(out_ref.dtype)
                out_ref[place, :] = result
                if split:
                    wide[place, :] = result.astype(jnp.float32)
        if split:
            rows_to_pieces(wide, pieces_ref, blocks, size, owners)

    out_shape = [jax.ShapeDtypeStruct(queries.shape, queries.dtype)]
    out_specs = [pl.BlockSpec(queries.shape, lambda i, *_: (0, 0))]
    scratch = [
        pltpu.VMEM((owners * far, cols), jnp.float32),
        pltpu.VMEM((owners * far, cols), jnp.float32),
        pltpu.VMEM(arrived.shape, arrived.dtype),
        pltpu.VMEM(queries.shape, queries.dtype),
        pltpu.VMEM((number, blocks, len(FAR), rows, size), far_tiles[0].dtype),
        pltpu.VMEM((blocks, size, cols), jnp.float32),
        pltpu.SemaphoreType.DMA((4, number)),
    ]
    if split:
        shape = (owners, size // owners * blocks, cols)
        out_shape.append(jax.ShapeDtypeStruct(shape, queries.dtype))
        out_specs.append(pl.BlockSpec(shape, lambda i, *_: (0, 0, 0)))
        scratch.append(pltpu.VMEM(queries.shape, jnp.float32))
    return pl.pallas_call(
        kernel,
        out_shape=out_shape,
        grid_spec=pltpu.PrefetchScalarGridSpec(
            num_scalar_prefetch=2,
            grid=(1,),
            in_specs=[HBM] * (number + len(partials) + 2),
            out_specs=out_specs,
            scratch_shapes=scratch,
        ),
        compiler_params=pltpu.CompilerParams(vmem_limit_bytes=LIMIT),
        cost_estimate=pl.CostEstimate(
            flops=4 * blocks * size * size * cols, bytes_accessed=4 << 20, transcendentals=0
        ),
        name="add_far",
    )(offsets, counts, *in_hbm(far_tiles), *in_hbm(partials), arrived, *in_hbm([queries]))


def on_device(affinity_tiles, block_ids, valid_counts, queries):
    blocks, slots = block_ids.shape
    rows, size = affinity_tiles.shape[2:]
    cols = queries.shape[1]
    owners = lax.axis_size("db")
    first_block = lax.axis_index("db") * blocks
    count = lax.axis_size("pb")
    forth = [(i, (i + 1) % count) for i in range(count)]
    back = [((i + 1) % count, i) for i in range(count)]
    opposite = [(i, (i + 2) % count) for i in range(count)]
    before = lax.ppermute(affinity_tiles, "pb", forth)
    after = lax.ppermute(affinity_tiles, "pb", back)
    across_far = lax.ppermute(affinity_tiles[:, FAR[0] : FAR[-1] + 1], "pb", opposite)
    far_tiles = [affinity_tiles, before, after, across_far]
    place = lax.axis_index("pb")
    offsets = jnp.stack([(place + shift) % count * rows for shift in (0, -1, 1, 2)])
    near_index = jnp.clip(block_ids - first_block + EDGE, 0, blocks + 2 * EDGE - 1)
    far = block_ids[:, FAR[0] : FAR[-1] + 1].reshape(1, -1)
    slots = far.shape[1]
    digits = jnp.concatenate([far // BASE, far % BASE], axis=1).astype(jnp.float32)
    digits = jnp.pad(digits, ((0, 0), (0, cols - 2 * slots)))
    up = [(i, i + 1) for i in range(owners - 1)]
    down = [(i + 1, i) for i in range(owners - 1)]
    ranking, wanted = queries, None
    pieces = split_blocks(queries, digits, blocks, size, owners)
    for step in range(ITERS):
        own = ranking.reshape(blocks, size, cols)
        held = lax.all_to_all(pieces, "db", split_axis=0, concat_axis=0, tiled=True)
        low = lax.ppermute(own[blocks - EDGE :], "db", up)
        high = lax.ppermute(own[:EDGE], "db", down)
        beyond = lax.ppermute(own, "pb", opposite)
        if wanted is None:
            chosen, wanted = select_pieces(held, slots, [low, high])
        else:
            (chosen,) = select_pieces(held, slots, [low, high, beyond], wanted)
        arrived = lax.all_to_all(
            chosen.reshape(owners, slots, -1), "db", split_axis=0, concat_axis=0, tiled=True
        ).reshape(chosen.shape)
        reach = [lax.ppermute(low, "pb", opposite), beyond, lax.ppermute(high, "pb", opposite)]
        product = near_product(near_index, valid_counts, [(affinity_tiles,)], reach)
        product, sides = lax.optimization_barrier((product, (before, after)))
        quarters = [(affinity_tiles,), (sides[0],), (sides[1],)]
        partials = [
            near_product(near_index, valid_counts, quarters, [low, own, high]),
            lax.ppermute(product, "pb", opposite),
        ]
        done = add_far(offsets, valid_counts, far_tiles, arrived, partials, queries, owners, step < ITERS - 1)
        ranking = done[0]
        pieces = done[-1]
    return ranking


def solution(mesh):
    return jax.shard_map(
        on_device,
        mesh=mesh,
        in_specs=(P("db", None, "pb", None), P("db", None), P("db"), P("db", "pb")),
        out_specs=P("db", "pb"),
        check_vma=False,
    )
```

```python
import jax
import jax.numpy as jnp
from jax import lax
from jax.experimental import pallas as pl
from jax.experimental.pallas import tpu as pltpu
from jax.sharding import PartitionSpec as P

EDGE = 2
ITERS = 2
BASE = 256
FAR = (1, 2)
VMEM = pl.BlockSpec(memory_space=pltpu.VMEM)
HBM = pl.BlockSpec(memory_space=pltpu.HBM)
LIMIT = 12 << 20


def in_hbm(arrays):
    return [pltpu.with_memory_space_constraint(array, pltpu.HBM) for array in arrays]


def rows_to_pieces(wide, pieces_ref, blocks, size, owners):
    for k in range(owners):
        for part in range(size // owners):
            rows = wide[pl.ds(part * owners + k, blocks, stride=size), :]
            pieces_ref[k, part * blocks : (part + 1) * blocks, :] = rows.astype(pieces_ref.dtype)


def split_blocks(queries, digits, blocks, size, owners):
    cols = queries.shape[1]
    rows = size // owners * blocks

    def kernel(q_ref, digits_ref, pieces_ref, wide):
        wide[...] = q_ref[...].astype(jnp.float32)
        rows_to_pieces(wide, pieces_ref, blocks, size, owners)
        for k in range(owners):
            pieces_ref[k, rows:, :] = jnp.broadcast_to(digits_ref[...], (8, cols)).astype(pieces_ref.dtype)

    return pl.pallas_call(
        kernel,
        out_shape=jax.ShapeDtypeStruct((owners, rows + 8, cols), queries.dtype),
        in_specs=[VMEM, VMEM],
        out_specs=VMEM,
        scratch_shapes=[pltpu.VMEM(queries.shape, jnp.float32)],
        name="split_blocks",
    )(queries, digits)


def select_pieces(held, slots, after, wanted=None):
    devices, height, cols = held.shape
    blocks = height // 16 * 8
    parts = 2
    block_total = devices * blocks
    group = 8

    def kernel(held_ref, *rest):
        rest = rest[len(after) :]
        if wanted is None:
            out_ref, wanted_out, flat = rest
            digits = held_ref[:, parts * blocks :, :].astype(jnp.float32)[:, 0, :].T
            ids = (digits[:slots] * BASE + digits[slots : 2 * slots]).astype(jnp.int32)
            wanted_out[...] = ids
        else:
            wanted_ref, out_ref, flat = rest
            ids = wanted_ref[...]
        for s in range(devices):
            for part in range(parts):
                flat[s * blocks : (s + 1) * blocks, part * cols : (part + 1) * cols] = held_ref[
                    s, part * blocks : (part + 1) * blocks, :
                ]
        column = lax.broadcasted_iota(jnp.int32, (slots, block_total), 1)
        for first in range(0, devices, group):
            hits = [
                jnp.where(
                    jnp.broadcast_to(ids[:, d : d + 1], (slots, block_total)) == column, 1.0, 0.0
                ).astype(held.dtype)
                for d in range(first, first + group)
            ]
            out_ref[first * slots : (first + group) * slots, :] = jnp.dot(
                jnp.concatenate(hits, axis=0), flat[...], preferred_element_type=jnp.float32
            ).astype(out_ref.dtype)

    out_shape = [jax.ShapeDtypeStruct((devices * slots, parts * cols), held.dtype)]
    if wanted is None:
        out_shape.append(jax.ShapeDtypeStruct((slots, devices), jnp.int32))
    operands = () if wanted is None else (wanted,)
    return pl.pallas_call(
        kernel,
        out_shape=out_shape,
        in_specs=[VMEM] + [HBM] * len(after) + [VMEM] * len(operands),
        out_specs=[VMEM] * len(out_shape),
        scratch_shapes=[pltpu.VMEM((block_total, parts * cols), held.dtype)],
        compiler_params=pltpu.CompilerParams(vmem_limit_bytes=LIMIT),
        cost_estimate=pl.CostEstimate(
            flops=2 * devices * slots * block_total * parts * cols, bytes_accessed=2 << 20, transcendentals=0
        ),
        name="select_pieces",
    )(held, *in_hbm(after), *operands)


def near_product(near_index, counts, quarters, reach):
    blocks, _, rows, size = quarters[0][0].shape
    slots = near_index.shape[1]
    cols = reach[0].shape[2]
    dtype = reach[0].dtype
    group = 4
    number = len(quarters)
    near = [t for t in range(slots) if t not in FAR]
    flat = [part for quarter in quarters for part in quarter]

    def kernel(index_ref, count_ref, *refs):
        parts = iter(refs)
        tiles = [[next(parts) for _ in quarter] for quarter in quarters]
        *reach_refs, out_ref, panels, sems = parts
        step = pl.program_id(0)

        @pl.when(step == 0)
        def _():
            copies, first = [], 0
            for n, (ref, array) in enumerate(zip(reach_refs, reach)):
                target = panels.at[first : first + array.shape[0]]
                copies.append(pltpu.make_async_copy(ref, target, sems.at[n]))
                first += array.shape[0]
            for copy in copies:
                copy.start()
            for copy in copies:
                copy.wait()

        for r in range(group):
            b = step * group + r
            total = jnp.zeros((number * rows, cols), jnp.float32)
            for first in range(0, len(near), 2):
                left, right = [], []
                for t in near[first : first + 2]:
                    tile = jnp.concatenate(
                        [quarter[t * len(quarter) // slots][r, t % (slots // len(quarter))] for quarter in tiles],
                        axis=0,
                    )
                    left.append(jnp.where(t < count_ref[b], tile, jnp.zeros_like(tile)))
                    right.append(panels[index_ref[b, t]])
                total += jnp.dot(
                    jnp.concatenate(left, axis=1),
                    jnp.concatenate(right, axis=0),
                    preferred_element_type=jnp.float32,
                )
            out_ref[r] = total

    return pl.pallas_call(
        kernel,
        out_shape=jax.ShapeDtypeStruct((blocks, number * rows, cols), jnp.float32),
        grid_spec=pltpu.PrefetchScalarGridSpec(
            num_scalar_prefetch=2,
            grid=(blocks // group,),
            in_specs=[
                pl.BlockSpec((group,) + part.shape[1:], lambda i, *_: (i, 0, 0, 0)) for part in flat
            ]
            + [HBM] * len(reach),
            out_specs=pl.BlockSpec((group, number * rows, cols), lambda i, *_: (i, 0, 0)),
            scratch_shapes=[
                pltpu.VMEM((blocks + 2 * EDGE, size, cols), dtype),
                pltpu.SemaphoreType.DMA((len(reach),)),
            ],
        ),
        compiler_params=pltpu.CompilerParams(vmem_limit_bytes=LIMIT),
        cost_estimate=pl.CostEstimate(
            flops=2 * blocks * len(near) * number * rows * size * cols,
            bytes_accessed=number << 21,
            transcendentals=0,
        ),
        name="near_product",
    )(near_index, counts, *flat, *in_hbm(reach))


def add_far(offsets, counts, far_tiles, arrived, partials, queries, owners, split):
    blocks, _, rows, size = far_tiles[0].shape
    cols = queries.shape[1]
    far = arrived.shape[0] // owners
    number = len(far_tiles)

    def kernel(offset_ref, count_ref, *refs):
        tile_refs, partial_refs = refs[:number], refs[number : number + len(partials)]
        arrived_ref, q_ref, out_ref = refs[number + len(partials) : number + len(partials) + 3]
        rest = refs[number + len(partials) + 3 :]
        if split:
            pieces_ref, upper, lower, landed, q_rows, tiles, sums, sems, wide = rest
        else:
            upper, lower, landed, q_rows, tiles, sums, sems = rest
        chunks = [slice(c * owners * far // number, (c + 1) * owners * far // number) for c in range(number)]
        landings = [
            pltpu.make_async_copy(arrived_ref.at[rows_of], landed.at[rows_of], sems.at[2, c])
            for c, rows_of in enumerate(chunks)
        ]
        for copy in landings:
            copy.start()
        copies = [
            pltpu.make_async_copy(
                ref if part.shape[1] == len(FAR) else ref.at[:, FAR[0] : FAR[-1] + 1], tiles.at[n], sems.at[0, n]
            )
            for n, (ref, part) in enumerate(zip(tile_refs, far_tiles))
        ]
        first = 0
        for n, (ref, part) in enumerate(zip(partial_refs, partials)):
            copies.append(
                pltpu.make_async_copy(ref, sums.at[:, first : first + part.shape[1]], sems.at[1, n])
            )
            first += part.shape[1]
        copies.append(pltpu.make_async_copy(q_ref, q_rows, sems.at[3, 0]))
        for copy in copies:
            copy.start()
        for copy, rows_of in zip(landings, chunks):
            copy.wait()
            upper[rows_of, :] = landed[rows_of, :cols].astype(jnp.float32)
            lower[rows_of, :] = landed[rows_of, cols:].astype(jnp.float32)
        for copy in copies:
            copy.wait()
        for b in range(blocks):
            left, right = [], []
            for s, t in enumerate(FAR):
                tile = tiles[:, b, s].reshape(size, size)
                left.append(jnp.where(t < count_ref[b], tile, jnp.zeros_like(tile)))
                for half in (upper, lower):
                    right.append(half[pl.ds(2 * b + s, owners, stride=far), :].astype(queries.dtype))
            total = sums[b] + jnp.dot(
                jnp.concatenate(left, axis=1),
                jnp.concatenate(right, axis=0),
                preferred_element_type=jnp.float32,
            )
            for n in range(number):
                place = pl.ds(pl.multiple_of(b * size + offset_ref[n], rows), rows)
                result = 0.99 * total[n * rows : (n + 1) * rows] + q_rows[place, :].astype(jnp.float32)
                result = result.astype(out_ref.dtype)
                out_ref[place, :] = result
                if split:
                    wide[place, :] = result.astype(jnp.float32)
        if split:
            rows_to_pieces(wide, pieces_ref, blocks, size, owners)

    out_shape = [jax.ShapeDtypeStruct(queries.shape, queries.dtype)]
    out_specs = [pl.BlockSpec(queries.shape, lambda i, *_: (0, 0))]
    scratch = [
        pltpu.VMEM((owners * far, cols), jnp.float32),
        pltpu.VMEM((owners * far, cols), jnp.float32),
        pltpu.VMEM(arrived.shape, arrived.dtype),
        pltpu.VMEM(queries.shape, queries.dtype),
        pltpu.VMEM((number, blocks, len(FAR), rows, size), far_tiles[0].dtype),
        pltpu.VMEM((blocks, size, cols), jnp.float32),
        pltpu.SemaphoreType.DMA((4, number)),
    ]
    if split:
        shape = (owners, size // owners * blocks, cols)
        out_shape.append(jax.ShapeDtypeStruct(shape, queries.dtype))
        out_specs.append(pl.BlockSpec(shape, lambda i, *_: (0, 0, 0)))
        scratch.append(pltpu.VMEM(queries.shape, jnp.float32))
    return pl.pallas_call(
        kernel,
        out_shape=out_shape,
        grid_spec=pltpu.PrefetchScalarGridSpec(
            num_scalar_prefetch=2,
            grid=(1,),
            in_specs=[HBM] * (number + len(partials) + 2),
            out_specs=out_specs,
            scratch_shapes=scratch,
        ),
        compiler_params=pltpu.CompilerParams(vmem_limit_bytes=LIMIT),
        cost_estimate=pl.CostEstimate(
            flops=4 * blocks * size * size * cols, bytes_accessed=4 << 20, transcendentals=0
        ),
        name="add_far",
    )(offsets, counts, *in_hbm(far_tiles), *in_hbm(partials), arrived, *in_hbm([queries]))


def on_device(affinity_tiles, block_ids, valid_counts, queries):
    blocks, slots = block_ids.shape
    rows, size = affinity_tiles.shape[2:]
    cols = queries.shape[1]
    owners = lax.axis_size("db")
    first_block = lax.axis_index("db") * blocks
    count = lax.axis_size("pb")
    forth = [(i, (i + 1) % count) for i in range(count)]
    back = [((i + 1) % count, i) for i in range(count)]
    opposite = [(i, (i + 2) % count) for i in range(count)]
    before = lax.ppermute(affinity_tiles, "pb", forth)
    after = lax.ppermute(affinity_tiles, "pb", back)
    across_far = lax.ppermute(affinity_tiles[:, FAR[0] : FAR[-1] + 1], "pb", opposite)
    far_tiles = [affinity_tiles, before, after, across_far]
    place = lax.axis_index("pb")
    offsets = jnp.stack([(place + shift) % count * rows for shift in (0, -1, 1, 2)])
    near_index = jnp.clip(block_ids - first_block + EDGE, 0, blocks + 2 * EDGE - 1)
    far = block_ids[:, FAR[0] : FAR[-1] + 1].reshape(1, -1)
    slots = far.shape[1]
    digits = jnp.concatenate([far // BASE, far % BASE], axis=1).astype(jnp.float32)
    digits = jnp.pad(digits, ((0, 0), (0, cols - 2 * slots)))
    up = [(i, i + 1) for i in range(owners - 1)]
    down = [(i + 1, i) for i in range(owners - 1)]
    ranking, wanted = queries, None
    pieces = split_blocks(queries, digits, blocks, size, owners)
    for step in range(ITERS):
        own = ranking.reshape(blocks, size, cols)
        held = lax.all_to_all(pieces, "db", split_axis=0, concat_axis=0, tiled=True)
        low = lax.ppermute(own[blocks - EDGE :], "db", up)
        high = lax.ppermute(own[:EDGE], "db", down)
        beyond = lax.ppermute(own, "pb", opposite)
        if wanted is None:
            chosen, wanted = select_pieces(held, slots, [low, high])
        else:
            (chosen,) = select_pieces(held, slots, [low, high, beyond], wanted)
        arrived = lax.all_to_all(
            chosen.reshape(owners, slots, -1), "db", split_axis=0, concat_axis=0, tiled=True
        ).reshape(chosen.shape)
        reach = [lax.ppermute(low, "pb", opposite), beyond, lax.ppermute(high, "pb", opposite)]
        product = near_product(near_index, valid_counts, [(affinity_tiles,)], reach)
        product, sides = lax.optimization_barrier((product, (before, after)))
        quarters = [[(affinity_tiles,)], [(sides[0],), (sides[1],)]]
        if step > 0:
            quarters = [quarters[0] + quarters[1]]
        partials = [near_product(near_index, valid_counts, part, [low, own, high]) for part in quarters]
        partials.append(lax.ppermute(product, "pb", opposite))
        done = add_far(offsets, valid_counts, far_tiles, arrived, partials, queries, owners, step < ITERS - 1)
        ranking = done[0]
        pieces = done[-1]
    return ranking


def solution(mesh):
    return jax.shard_map(
        on_device,
        mesh=mesh,
        in_specs=(P("db", None, "pb", None), P("db", None), P("db"), P("db", "pb")),
        out_specs=P("db", "pb"),
        check_vma=False,
    )
```
